32 devices in a mesh: ctx: 8 (over z, core), fsdp: 4 (over y, x).
Axes of the slice: x: 2, y: 2, z: 4, core: 2. Of those that a mesh axis runs over, the one named last changes fastest.
Arguments:
- tokens: bfloat16 [4, 1024, 2048], P('fsdp', 'ctx'), may hold values from -6 to 6
- cotangent: bfloat16 [4, 1024, 2048], P('fsdp', 'ctx'), may hold values from -6 to 6
- lengths: int32 [4, 4], P('fsdp'), may hold values from 1 to 768, 1024 in all within a row
- span_order: int32 [4, 16], P('fsdp'), may hold values from 0 to 15, each once within a row
- gain_attn: bfloat16 [2048], P('fsdp'), may hold values from 0.5 to 1.5
- w_query: bfloat16 [2048, 2048], P('fsdp'), may hold values from -0.1875 to 0.1875
- w_key: bfloat16 [2048, 256], P('fsdp'), may hold values from -0.1875 to 0.1875
- w_value: bfloat16 [2048, 256], P('fsdp'), may hold values from -0.125 to 0.125
- w_out: bfloat16 [2048, 2048], P('fsdp'), may hold values from -0.5 to 0.5
- gain_ffn: bfloat16 [2048], P('fsdp'), may hold values from 0.5 to 1.5
- w_gate: bfloat16 [2048, 5632], P('fsdp'), may hold values from -0.125 to 0.125
- w_up: bfloat16 [2048, 5632], P('fsdp'), may hold values from -0.125 to 0.125
- w_down: bfloat16 [5632, 2048], P('fsdp'), may hold values from -0.078125 to 0.078125
Outputs:
- output: bfloat16 [4, 1024, 2048], P('fsdp', 'ctx')
- grad_tokens: bfloat16 [4, 1024, 2048], P('fsdp', 'ctx')
- grad_gain_attn: float32 [2048], P(('ctx', 'fsdp'))
- grad_query: float32 [2048, 2048], P(('ctx', 'fsdp'))
- grad_key: float32 [2048, 256], P(('ctx', 'fsdp'))
- grad_value: float32 [2048, 256], P(('ctx', 'fsdp'))
- grad_out: float32 [2048, 2048], P(('ctx', 'fsdp'))
- grad_gain_ffn: float32 [2048], P(('ctx', 'fsdp'))
- grad_gate: float32 [2048, 5632], P(('ctx', 'fsdp'))
- grad_up: float32 [2048, 5632], P(('ctx', 'fsdp'))
- grad_down: float32 [5632, 2048], P(('ctx', 'fsdp'))
The draws below stay inside these ranges and needn't reach their ends.
Inputs may be any that keep to these rules, and one draw needn't show every extreme that they name: `lengths`: each row sums to 1024, and its largest entry is exactly 768. `span_order`: each row is a permutation of the 16 spans of its pack.
All inputs are finite; a program needn't handle non-finite values.
Results may differ from the reference program's by a relative error of at most 0.015.
Values may be sent and summed in bfloat16 or wider, within the bound.
No kernel may reach another device: no remote copies, remote signals or barrier semaphores. Data moves between devices by JAX's collectives and lax.ppermute only.
A program may use at most 384 MiB of HBM per device.

```python
import math
import jax
import jax.numpy as jnp
import numpy as np
from jax import lax

D = 2048
HEADS = 32
KV_HEADS = 4
HEAD = 64
FF = 5632
TOK_DEV = 128
NSEQ = 4
GROUPS = 4
GROUP_TOKENS = 1024
LONGEST = 768
SLOTS = 16
KV_WIDTH = 256
N_CTX = 8


def steps_of(rng, dims, split, low, largest):
    level = 1.0
    for position, blocks in split:
        heights = jax.random.uniform(jax.random.fold_in(jax.random.fold_in(rng, 6), position), (blocks,), jnp.float32, low / len(split), largest / len(split))
        level = level * jnp.repeat(jnp.exp(heights), dims[position] // blocks).reshape((-1,) + (1,) * (len(dims) - 1 - position))
    return level


def profile(number_of, total, reach, skew):
    portions = [(1 << 20) // math.isqrt(rank ** skew) + 1 for rank in range(2, number_of + 1)]
    surplus, holding = total - reach - (number_of - 1), [1] * (number_of - 1)
    while surplus > 0:
        free = [i for i in range(number_of - 1) if holding[i] < reach]
        pool, remaining = sum([portions[i] for i in free]), surplus
        for i in free:
            extra = min(reach - holding[i], max(1, remaining * portions[i] // pool), surplus)
            holding[i] = holding[i] + extra
            surplus = surplus - extra
    return np.array([reach] + holding)


def ragged_sizes(own_key, number_of, total, reach, lean):
    if number_of == 2:
        one = jax.random.randint(own_key, (), max(1, total - reach), min(reach, total - 1) + 1)
        return jnp.stack([one, total - one])
    tallies = jnp.asarray(profile(number_of, total, reach, lean), jnp.int32)
    pairs = (number_of - 1) // 2
    giver, sink = tallies[1:1 + 2 * pairs:2], tallies[2:2 + 2 * pairs:2]
    slack = jnp.minimum(giver - 1, reach - sink)
    moved = jax.random.randint(jax.random.fold_in(own_key, 1), (pairs,), 0, 1 << 20) % (slack + 1)
    tallies = tallies.at[1:1 + 2 * pairs:2].set(giver - moved).at[2:2 + 2 * pairs:2].set(sink + moved)
    return tallies[jax.random.permutation(jax.random.fold_in(own_key, 2), number_of)]


def centred(rng, shape, width, most, cuts=(), held_as=jnp.bfloat16):
    array = jax.random.normal(rng, shape, jnp.float32) * width
    if len(cuts) > 0:
        array = steps_of(rng, shape, cuts, -0.22, 0.18) * array
    return jnp.clip(array, min=-most, max=most).astype(held_as)


def setup_inputs(seed: int = 0) -> dict:
    key_list = jax.random.split(jax.random.key(seed), 14)
    return {
        "tokens": centred(key_list[0], (GROUPS, GROUP_TOKENS, D), 1.0, 6.0, ((0, 4), (1, 8))),
        "cotangent": centred(key_list[1], (GROUPS, GROUP_TOKENS, D), 1.0, 6.0, ((0, 4), (1, 8))),
        "lengths": jax.vmap(lambda own: ragged_sizes(own, NSEQ, GROUP_TOKENS, LONGEST, 2))(jax.random.split(key_list[2], GROUPS)).reshape((GROUPS, NSEQ)).astype(jnp.int32),
        "span_order": jax.vmap(lambda own: jax.random.permutation(own, SLOTS))(jax.random.split(key_list[3], GROUPS)).reshape((GROUPS, SLOTS)).astype(jnp.int32),
        "gain_attn": jnp.clip(1.0 + 0.1 * jax.random.normal(key_list[4], (D,), jnp.float32), 0.5, 1.5).astype(jnp.bfloat16),
        "w_query": centred(key_list[5], (D, D), (D // 2) ** -0.5, 0.1875, ((0, 4),)),
        "w_key": centred(key_list[6], (D, KV_WIDTH), (D // 2) ** -0.5, 0.1875, ((0, 4),)),
        "w_value": centred(key_list[7], (D, KV_WIDTH), D ** -0.5, 0.125, ((0, 4),)),
        "w_out": centred(key_list[8], (D, D), (D // 16) ** -0.5, 0.5, ((0, 4),)),
        "gain_ffn": jnp.clip(1.0 + 0.1 * jax.random.normal(key_list[9], (D,), jnp.float32), 0.5, 1.5).astype(jnp.bfloat16),
        "w_gate": centred(key_list[10], (D, FF), D ** -0.5, 0.125, ((0, 4),)),
        "w_up": centred(key_list[11], (D, FF), D ** -0.5, 0.125, ((0, 4),)),
        "w_down": centred(key_list[12], (FF, D), FF ** -0.5, 0.078125, ((0, 4),)),
    }


EPS = 1e-05
THETA = 10000.0
NEGATIVE = -1e+30

@jax.custom_vjp
def low(v):
    return lax.optimization_barrier(v.astype(jnp.bfloat16)).astype(jnp.float32)

@jax.custom_vjp
def low_back(v):
    return v

def low_keep(v):
    return (low(v), None)

def low_pass(kept, grad):
    return (grad,)

def back_keep(v):
    return (v, None)

def back_low(kept, grad):
    return (low(grad),)
low.defvjp(low_keep, low_pass)
low_back.defvjp(back_keep, back_low)

def highest(left, right):
    return jnp.dot(left, right, precision=lax.Precision.HIGHEST)

def rms_norm(values, gain):
    return values * lax.rsqrt(lax.optimization_barrier(jnp.mean(values * values, axis=-1, keepdims=True)) + EPS) * gain

def token_meta(length_row, dealt_order):
    span_rows = TOK_DEV // 2
    row_ids = jnp.arange(TOK_DEV * N_CTX, dtype=jnp.int32)
    anchor = dealt_order[row_ids // span_rows].astype(jnp.int32) * span_rows + row_ids % span_rows
    seq_ends = jnp.cumsum(length_row).astype(jnp.int32)
    segment = lax.optimization_barrier(jnp.sum((anchor[:, None] >= seq_ends[None, :]).astype(jnp.int32), axis=1)).astype(jnp.int32)
    seq_starts = (seq_ends - length_row).astype(jnp.int32)
    return ((anchor - seq_starts[segment]).astype(jnp.int32), segment)

def rope_tables(positions):
    half_dim = HEAD // 2
    inverse = THETA ** (-(jnp.arange(half_dim, dtype=jnp.float32) * 2.0 / HEAD))
    angles = positions.astype(jnp.float32)[:, None] * inverse[None, :]
    return (jnp.cos(angles)[:, None, :], jnp.sin(angles)[:, None, :])

def rotate(values, cosine, sine_table):
    half_dim = values.shape[-1] // 2
    front_half, back_half = (values[..., :half_dim], values[..., half_dim:])
    return jnp.concatenate([front_half * cosine - back_half * sine_table, back_half * cosine + front_half * sine_table], axis=-1)

def group_forward(inputs, positions, segments, gain_one, w_query, w_key, w_value, w_out, gain_two, w_gate, w_up, w_down):
    group_rows = inputs.shape[0]
    group_heads = HEADS // KV_HEADS
    score_scale = HEAD ** (-0.5)
    cosine, sine_table = rope_tables(positions)
    normed_one = low(rms_norm(inputs, gain_one))
    queries = low(rotate(low_back(highest(normed_one, w_query)).reshape(group_rows, HEADS, HEAD), cosine, sine_table))
    keys = low(rotate(low_back(highest(normed_one, w_key)).reshape(group_rows, KV_HEADS, HEAD), cosine, sine_table))
    values = low(low_back(highest(normed_one, w_value))).reshape(group_rows, KV_HEADS, HEAD)
    allowed = (segments[:, None] == segments[None, :]) & (positions[None, :] <= positions[:, None])
    query_heads = queries.reshape(group_rows, KV_HEADS, group_heads, HEAD).transpose(1, 2, 0, 3)

    def one_head(operands):
        query_block, key_block, value_block = operands
        raw = jnp.einsum('gtd,sd->gts', query_block, key_block, precision=lax.Precision.HIGHEST)
        scores = low_back(jnp.where(allowed[None], score_scale * raw, NEGATIVE))
        row_max = lax.optimization_barrier(jnp.max(scores, axis=-1, keepdims=True))
        log_norm = row_max + jnp.log(lax.optimization_barrier(jnp.sum(jnp.exp(scores - row_max), axis=-1, keepdims=True)))
        weights = low(jnp.exp(scores - log_norm))
        return jnp.einsum('gts,sd->gtd', weights, value_block, precision=lax.Precision.HIGHEST)
    heads_out = lax.map(jax.checkpoint(one_head), (query_heads, keys.transpose(1, 0, 2), values.transpose(1, 0, 2)))
    attended = low(low_back(heads_out.transpose(2, 0, 1, 3).reshape(group_rows, HEADS * HEAD)))
    hidden_in = inputs + low_back(highest(attended, w_out))
    normed_two = low(rms_norm(hidden_in, gain_two))
    gate_lin = low_back(highest(normed_two, w_gate))
    up_lin = low_back(highest(normed_two, w_up))
    activated = low(jax.nn.silu(gate_lin) * up_lin)
    return hidden_in + highest(activated, w_down)

def reference(tokens, cotangent, lengths, span_order, gain_attn, w_query, w_key, w_value, w_out, gain_ffn, w_gate, w_up, w_down):
    positions, segments = jax.vmap(token_meta)(lengths, span_order)
    params = tuple((weight_arg.astype(jnp.float32) for weight_arg in (gain_attn, w_query, w_key, w_value, w_out, gain_ffn, w_gate, w_up, w_down)))

    def forward(inputs, *weights_all):

        def per_pack(operands):
            pack_rows, pack_pos, pack_seg = operands
            return group_forward(pack_rows, pack_pos, pack_seg, *weights_all)
        return lax.map(per_pack, (inputs, positions, segments))
    output, pullback = jax.vjp(forward, tokens.astype(jnp.float32), *params)
    grads = pullback(cotangent.astype(jnp.float32))
    return (output.astype(jnp.bfloat16), grads[0].astype(jnp.bfloat16), grads[1], grads[2], grads[3], grads[4], grads[5], grads[6], grads[7], grads[8], grads[9])
```

```python
import math

import jax
import jax.numpy as jnp
from jax import lax
from jax.sharding import PartitionSpec as P

HEADS = 32
KV_HEADS = 4
HEAD = 64
EPS = 1e-05
THETA = 10000.0
NEGATIVE = -1e30
BF = jnp.bfloat16
F32 = jnp.float32


def dot(left, right, dims, out=F32):
    return lax.dot_general(left, right, (dims, ((), ())), preferred_element_type=out)


def mm(left, right, out=F32):
    return dot(left, right, ((1,), (0,)), out)


def mm_nt(left, right, out=F32):
    return dot(left, right, ((1,), (1,)), out)


def mm_tn(left, right, out=F32):
    return dot(left, right, ((0,), (0,)), out)


def make_body(n_ctx, n_fsdp):
    nz = n_ctx // 2
    core_swap = [(i, i ^ 1) for i in range(n_ctx)]

    def shift(step):
        return [(i, ((i // 2 + step) % nz) * 2 + i % 2) for i in range(n_ctx)]

    def swap(x):
        return lax.ppermute(x, "ctx", core_swap)

    def gather_ctx(x):
        parts = [x] + [lax.ppermute(x, "ctx", shift(k)) for k in range(1, nz)]
        mine = jnp.concatenate(parts, 0)
        return jnp.concatenate([mine, swap(mine)], 0)

    def reduce_ctx(partial):
        rows = partial.shape[0] // (2 * nz)
        half = nz * rows
        other = swap(partial[half:])
        pair = partial[:half].astype(F32) + other.astype(F32)
        total = pair[:rows]
        low = pair.astype(BF)
        for k in range(1, nz):
            total = total + lax.ppermute(
                low[k * rows : (k + 1) * rows], "ctx", shift(nz - k)
            ).astype(F32)
        return total

    def body(
        tokens,
        cotangent,
        lengths,
        span_order,
        gain_attn,
        w_query,
        w_key,
        w_value,
        w_out,
        gain_ffn,
        w_gate,
        w_up,
        w_down,
    ):
        c = lax.axis_index("ctx")
        f = lax.axis_index("fsdp")
        z = c // 2
        p = c % 2
        tok = tokens.shape[1]
        span = tok // 2
        width = tokens.shape[2]
        rows_all = n_ctx * tok
        q_cols = HEADS * HEAD // n_ctx
        heads = HEADS // n_ctx
        kv = c * KV_HEADS // n_ctx
        ff = w_gate.shape[1]
        ff_c = ff // n_ctx
        ff_b = ff_c // n_fsdp
        shard = w_query.shape[0]
        score_scale = 1.0 / math.sqrt(HEAD)

        row = jnp.arange(rows_all, dtype=jnp.int32)
        block = row // tok
        dealt_dev = ((z - block % nz) % nz) * 2 + (p ^ (block // nz))
        slot = dealt_dev * 2 + (row % tok) // span
        slot_table = jnp.arange(span_order.shape[1], dtype=jnp.int32)
        chosen = jnp.sum(
            jnp.where(slot[:, None] == slot_table[None, :], span_order[0][None, :], 0), axis=1
        )
        anchor = chosen * span + row % span
        ends = jnp.cumsum(lengths[0])
        starts = ends - lengths[0]
        segment = jnp.sum((anchor[:, None] >= ends[None, :]).astype(jnp.int32), axis=1)
        first = jnp.sum(
            jnp.where(
                segment[:, None] == jnp.arange(ends.shape[0], dtype=jnp.int32)[None, :],
                starts[None, :],
                0,
            ),
            axis=1,
        )
        pos = anchor - first
        half_dim = HEAD // 2
        inverse = THETA ** (-(jnp.arange(half_dim, dtype=F32) * 2.0 / HEAD))
        angles = pos.astype(F32)[:, None] * inverse[None, :]
        cosine = jnp.cos(angles)[:, None, :]
        sine = jnp.sin(angles)[:, None, :]
        allowed = (segment[:, None] == segment[None, :]) & (pos[None, :] <= pos[:, None])

        def rotate(v, sign):
            a, b = v[..., :half_dim], v[..., half_dim:]
            return jnp.concatenate(
                [a * cosine - sign * b * sine, b * cosine + sign * a * sine], axis=-1
            )

        g1 = gain_attn.astype(F32)[:, None]
        g2 = gain_ffn.astype(F32)[:, None]

        def cols(w, start, size):
            return lax.dynamic_slice_in_dim(w, start, size, 1)

        wq = cols(w_query, c * q_cols, q_cols)
        wk = cols(w_key, kv * HEAD, HEAD)
        wv = cols(w_value, kv * HEAD, HEAD)
        wqkv_loc = (jnp.concatenate([wq, wk, wv], 1).astype(F32) * g1).astype(BF)
        pad = wqkv_loc.shape[1]
        gains = jnp.concatenate([gain_attn, gain_ffn])
        extra = 16
        gains = jnp.pad(gains, (0, extra * pad - gains.shape[0])).reshape(extra, pad)
        small = lax.all_gather(jnp.concatenate([wqkv_loc, gains], 0), "fsdp", axis=0)
        wqkv = small[:, :shard].reshape(width, pad)
        gains_all = small[:, shard:].reshape(n_fsdp, extra * pad)[:, : 2 * shard]
        gain1 = gains_all[:, :shard].reshape(width).astype(F32)
        gain2 = gains_all[:, shard:].reshape(width).astype(F32)

        wo = lax.all_gather(w_out, "fsdp", axis=0, tiled=True)
        wg = lax.all_gather(
            (cols(w_gate, c * ff_c, ff_c).astype(F32) * g2).astype(BF), "fsdp", axis=0, tiled=True
        )
        wu = lax.all_gather(
            (cols(w_up, c * ff_c, ff_c).astype(F32) * g2).astype(BF), "fsdp", axis=0, tiled=True
        )
        per_shard = w_down.shape[0] // ff_c
        source = c // per_shard
        inner = (c % per_shard) * ff_c
        wd_block = jnp.where(
            f == source, lax.dynamic_slice_in_dim(w_down, inner + f * ff_b, ff_b, 0), 0
        )
        for k in range(1, n_fsdp):
            send = lax.dynamic_slice_in_dim(
                w_down, inner + ((f + k) % n_fsdp) * ff_b, ff_b, 0
            )
            pairs = [
                (
                    ci * n_fsdp + ci // per_shard,
                    ci * n_fsdp + (ci // per_shard + k) % n_fsdp,
                )
                for ci in range(n_ctx)
            ]
            wd_block = wd_block + lax.ppermute(send, ("ctx", "fsdp"), pairs)
        wd = lax.all_gather(wd_block, "fsdp", axis=0, tiled=True)

        x = gather_ctx(tokens[0])
        cot = gather_ctx(cotangent[0])
        xf = x.astype(F32)
        r1 = lax.rsqrt(jnp.mean(xf * xf, axis=-1, keepdims=True) + EPS)
        qkv = mm(x, wqkv) * r1
        q = rotate(qkv[:, :q_cols].reshape(rows_all, heads, HEAD), 1.0).astype(BF)
        k = rotate(qkv[:, q_cols : q_cols + HEAD].reshape(rows_all, 1, HEAD), 1.0).astype(BF)[:, 0]
        v = qkv[:, q_cols + HEAD :].astype(BF)
        scores = jnp.einsum("thd,ud->htu", q, k, preferred_element_type=F32)
        scores = jnp.where(allowed[None], scores * score_scale, NEGATIVE)
        top = jnp.max(scores, axis=-1, keepdims=True)
        log_norm = top + jnp.log(jnp.sum(jnp.exp(scores - top), axis=-1, keepdims=True))
        probs = jnp.exp(scores - log_norm)
        weights = probs.astype(BF)
        att = jnp.einsum("htu,ud->thd", weights, v, preferred_element_type=F32)
        attended = att.astype(BF).reshape(rows_all, q_cols)

        same = jnp.concatenate(
            [attended], 0
        )
        def blocks(v2, b):
            return v2[b * tok : (b + 1) * tok]

        got = []
        for qq in range(2):
            for kk in range(nz):
                piece = blocks(attended, qq * nz + kk)
                perm = [
                    (i, ((i // 2 - kk) % nz) * 2 + ((i % 2) ^ qq)) for i in range(n_ctx)
                ]
                got.append(piece if (qq == 0 and kk == 0) else lax.ppermute(piece, "ctx", perm))
        full = jnp.stack(got, 0)
        order = jnp.arange(n_ctx, dtype=jnp.int32)
        pick = ((order % 2) ^ p) * nz + (order // 2 - z) % nz
        own_att = jnp.take(full, pick, axis=0).transpose(1, 0, 2).reshape(tok, width)
        inputs = tokens[0].astype(F32)
        hidden = inputs + mm(own_att, wo)
        r2_own = lax.rsqrt(jnp.mean(hidden * hidden, axis=-1, keepdims=True) + EPS)
        h = gather_ctx(hidden.astype(BF))
        hf = h.astype(F32)
        r2 = lax.rsqrt(jnp.mean(hf * hf, axis=-1, keepdims=True) + EPS)
        gate = mm(h, wg) * r2
        up = mm(h, wu) * r2
        sig = jax.nn.sigmoid(gate)
        act = (gate * sig * up).astype(BF)
        act_grad = mm_nt(cot, wd) * r2
        gg = (act_grad * up * sig * (1.0 + gate * (1.0 - sig))).astype(BF)
        ug = (act_grad * gate * sig).astype(BF)
        n2 = reduce_ctx((mm_nt(gg, wg) + mm_nt(ug, wu)).astype(BF))
        hidden_grad = (
            cotangent[0].astype(F32)
            + n2
            - hidden * (r2_own * r2_own * jnp.mean(n2 * hidden, axis=-1, keepdims=True))
        )
        branch = hidden_grad.astype(BF)
        branch_all = gather_ctx(branch)
        wo_c = lax.dynamic_slice_in_dim(wo, c * q_cols, q_cols, 0)
        agrad = mm_nt(branch_all, wo_c).astype(BF)
        output = (hidden + reduce_ctx(mm(act, wd).astype(BF))).astype(BF)

        ag3 = agrad.reshape(rows_all, heads, HEAD)
        pgrad = jnp.einsum("thd,ud->htu", ag3, v, preferred_element_type=F32)
        delta = jnp.sum(probs * pgrad, axis=-1, keepdims=True)
        sgrad = (probs * (pgrad - delta)).astype(BF)
        dq = jnp.einsum("htu,ud->thd", sgrad, k, preferred_element_type=F32) * score_scale
        dk = jnp.einsum("htu,thd->ud", sgrad, q, preferred_element_type=F32) * score_scale
        dv = jnp.einsum("htu,thd->ud", weights, ag3, preferred_element_type=F32)
        dqkv = jnp.concatenate(
            [
                rotate(dq, -1.0).reshape(rows_all, q_cols),
                rotate(dk[:, None, :], -1.0)[:, 0],
                dv,
            ],
            1,
        )
        dqkv = (dqkv * r1).astype(BF)
        n1 = reduce_ctx(mm_nt(dqkv, wqkv).astype(BF))
        r1_own = r1[:tok]
        grad_in = (
            hidden_grad
            + n1
            - inputs * (r1_own * r1_own * jnp.mean(n1 * inputs, axis=-1, keepdims=True))
        ).astype(BF)

        e_down = mm_tn(act, cot, BF)
        e_out = mm_tn(attended, branch_all, BF)
        e_cols = jnp.concatenate([mm_tn(h, gg, BF), mm_tn(h, ug, BF), mm_tn(x, dqkv, BF)], 1)
        rows_b = width // (n_ctx * n_fsdp)
        gd = lax.psum_scatter(e_down, "fsdp", scatter_dimension=0, tiled=True)
        go = lax.psum_scatter(e_out, "fsdp", scatter_dimension=0, tiled=True)
        ec = e_cols.reshape(n_ctx, n_fsdp, rows_b, e_cols.shape[1]).transpose(1, 0, 2, 3)
        ec = ec.reshape(n_fsdp, n_ctx * rows_b, e_cols.shape[1])
        ec = lax.psum_scatter(ec, "fsdp", scatter_dimension=0, tiled=True)[0]
        w_cols = jnp.concatenate([wg, wu, wqkv], 1).reshape(n_ctx, n_fsdp, rows_b, -1)
        w_mine = lax.dynamic_index_in_dim(w_cols, f, 1, keepdims=False)
        prod = ec.reshape(n_ctx, rows_b, -1).astype(F32) * w_mine.astype(F32)
        s2 = jnp.sum(prod[..., : 2 * ff_c], axis=-1, keepdims=True)
        s1 = jnp.sum(prod[..., 2 * ff_c :], axis=-1, keepdims=True)
        tail = jnp.concatenate([s1, s2, jnp.zeros((n_ctx, rows_b, 126), F32)], -1).astype(BF)
        ship = jnp.concatenate([ec.reshape(n_ctx, rows_b, -1), tail], -1)
        recv = lax.all_to_all(ship, "ctx", 0, 0, tiled=True)
        my_row = (c * n_fsdp + f) * rows_b
        gain1_r = lax.dynamic_slice_in_dim(gain1, my_row, rows_b, 0)
        gain2_r = lax.dynamic_slice_in_dim(gain2, my_row, rows_b, 0)
        recv = recv.astype(F32)

        def lay(start, size):
            return recv[:, :, start : start + size].transpose(1, 0, 2).reshape(rows_b, -1)

        grad_gate = lay(0, ff_c) * gain2_r[:, None]
        grad_up = lay(ff_c, ff_c) * gain2_r[:, None]
        grad_query = lay(2 * ff_c, q_cols) * gain1_r[:, None]
        share = n_ctx // KV_HEADS

        def lay_kv(start):
            part = recv[:, :, start : start + HEAD].reshape(KV_HEADS, share, rows_b, HEAD)
            return jnp.sum(part, 1).transpose(1, 0, 2).reshape(rows_b, -1) * gain1_r[:, None]

        grad_key = lay_kv(2 * ff_c + q_cols)
        grad_value = lay_kv(2 * ff_c + q_cols + HEAD)
        sums = jnp.sum(recv[:, :, -128:-126], 0)
        grad_g1 = sums[:, 0] / gain1_r
        grad_g2 = sums[:, 1] / gain2_r
        return (
            output[None],
            grad_in[None],
            grad_g1,
            grad_query,
            grad_key,
            grad_value,
            go.astype(F32),
            grad_g2,
            grad_gate,
            grad_up,
            gd.astype(F32),
        )

    return body


def solution(mesh):
    body = make_body(mesh.shape["ctx"], mesh.shape["fsdp"])
    both = ("ctx", "fsdp")
    in_specs = (
        P("fsdp", "ctx", None),
        P("fsdp", "ctx", None),
        P("fsdp", None),
        P("fsdp", None),
        P("fsdp"),
        P("fsdp", None),
        P("fsdp", None),
        P("fsdp", None),
        P("fsdp", None),
        P("fsdp"),
        P("fsdp", None),
        P("fsdp", None),
        P("fsdp", None),
    )
    out_specs = (
        P("fsdp", "ctx", None),
        P("fsdp", "ctx", None),
        P(both),
        P(both, None),
        P(both, None),
        P(both, None),
        P(both, None),
        P(both),
        P(both, None),
        P(both, None),
        P(both, None),
    )
    return jax.shard_map(body, mesh=mesh, in_specs=in_specs, out_specs=out_specs, check_vma=False)
```

```python
import functools
import math

import jax
import jax.numpy as jnp
from jax import lax
from jax.experimental import pallas as pl
from jax.experimental.pallas import tpu as pltpu
from jax.sharding import PartitionSpec as P

HEADS = 32
KV_HEADS = 4
HEAD = 64
EPS = 1e-05
THETA = 10000.0
NEGATIVE = -1e30
BF = jnp.bfloat16
F32 = jnp.float32
TILE = 256
VMEM = pl.BlockSpec(memory_space=pltpu.VMEM)
SMEM = pl.BlockSpec(memory_space=pltpu.SMEM)
ANY = pl.BlockSpec(memory_space=pl.ANY)


def dot(left, right, dims, out=F32):
    return lax.dot_general(left, right, (dims, ((), ())), preferred_element_type=out)


def mm(left, right, out=F32):
    return dot(left, right, ((1,), (0,)), out)


def mm_nt(left, right, out=F32):
    return dot(left, right, ((1,), (1,)), out)


def mm_tn(left, right, out=F32):
    return dot(left, right, ((0,), (0,)), out)


def params(mb):
    return pltpu.CompilerParams(vmem_limit_bytes=mb << 20)


def cost(flops, moved, trans=0):
    return pl.CostEstimate(flops=int(flops), bytes_accessed=int(moved), transcendentals=int(trans))


def norm_qkv_body(n_x, n_f, shard, ids, *refs):
    xs = refs[:n_x]
    packs = refs[n_x : n_x + n_f]
    normed, qkv, w_all, gains, row, sems = refs[n_x + n_f :]
    me = ids[0]
    copies = []
    for k in range(n_f):
        at = me ^ k
        copies.append(
            pltpu.make_async_copy(
                packs[k].at[pl.ds(0, shard)],
                w_all.at[pl.ds(pl.multiple_of(at * shard, shard), shard)],
                sems.at[k],
            )
        )
        copies.append(
            pltpu.make_async_copy(packs[k].at[pl.ds(shard, 16)], gains.at[at], sems.at[n_f + k])
        )
    for copy in copies:
        copy.start()
    for copy in copies:
        copy.wait()
    for g in range(n_f):
        part = gains[g].astype(F32)
        for j in range(shard // 128):
            start = g * shard + j * 128
            row[0:1, start : start + 128] = part[j : j + 1, 0:128]
    tok = xs[0].shape[0]
    gain = row[...]
    for b in range(n_x):
        x = xs[b][...].astype(F32)
        r = lax.rsqrt(jnp.mean(x * x, axis=-1, keepdims=True) + EPS)
        normed[b * tok : (b + 1) * tok, :] = (x * r * gain).astype(BF)
    qkv[...] = mm(normed[...], w_all[...])


def norm_qkv(f_id, xs, packs, shard):
    n_x, n_f = len(xs), len(packs)
    tok, width = xs[0].shape
    cols = packs[0].shape[1]
    rows = n_x * tok
    return pl.pallas_call(
        functools.partial(norm_qkv_body, n_x, n_f, shard),
        in_specs=[SMEM] + [VMEM] * n_x + [ANY] * n_f,
        out_specs=[VMEM] * 4,
        out_shape=[
            jax.ShapeDtypeStruct((rows, width), BF),
            jax.ShapeDtypeStruct((rows, cols), F32),
            jax.ShapeDtypeStruct((width, cols), BF),
            jax.ShapeDtypeStruct((n_f, 16, cols), BF),
        ],
        scratch_shapes=[pltpu.VMEM((1, width), F32), pltpu.SemaphoreType.DMA((2 * n_f,))],
        compiler_params=params(40),
        cost_estimate=cost(2 * rows * width * cols, 4 * rows * width),
        name="norm_qkv",
    )(f_id, *xs, *packs)


def half_swap(x):
    lane = lax.broadcasted_iota(jnp.int32, x.shape, 1)
    return jnp.where(
        lane % HEAD < HEAD // 2, pltpu.roll(x, 128 - HEAD // 2, 1), pltpu.roll(x, HEAD // 2, 1)
    )


def bias_rows(ends, n_seq, i, keys):
    t = i * TILE + lax.broadcasted_iota(jnp.int32, (1, TILE), 1)
    first = jnp.zeros((1, TILE), jnp.int32)
    for s in range(n_seq):
        first = jnp.where(t >= ends[s], ends[s], first)
    u = lax.broadcasted_iota(jnp.int32, (keys, TILE), 0)
    return jnp.where((u <= t) & (u >= first), 0.0, NEGATIVE)


def attention_body(
    span, heads, n_seq, offs, ends, qkv, cos, sin, att, qm, kk, vv, lse, v_t, att_s, bias
):
    rows = qkv.shape[0]
    n_span = rows // span
    pairs = heads // 2
    q_cols = heads * HEAD

    def prepare(i, _):
        src = pl.ds(pl.multiple_of(offs[i], span), span)
        dst = pl.ds(pl.multiple_of(i * span, span), span)
        c, s = cos[src, :], sin[src, :]
        low = lax.broadcasted_iota(jnp.int32, (span, 128), 1) < HEAD
        for pr in range(pairs):
            x = qkv[src, pr * 128 : (pr + 1) * 128]
            q = (x * c + half_swap(x) * s).astype(BF).astype(F32) * (1.0 / math.sqrt(HEAD))
            qm[2 * pr, dst, :] = jnp.where(low, q, 0.0).astype(BF)
            qm[2 * pr + 1, dst, :] = jnp.where(low, 0.0, q).astype(BF)
        x = qkv[src, q_cols : q_cols + 128]
        kv = x * jnp.where(low, c, 1.0) + half_swap(x) * jnp.where(low, s, 0.0)
        other = pltpu.roll(kv, HEAD, 1)
        kk[dst, :] = jnp.where(low, kv, other).astype(BF)
        vv[dst, :] = jnp.where(low, other, kv).astype(BF)
        return 0

    lax.fori_loop(0, n_span, prepare, 0)
    v_t[...] = jnp.transpose(vv[...].astype(F32))[0:HEAD, :].astype(BF)
    for i in range(rows // TILE):
        keys = (i + 1) * TILE
        bias[0:keys, :] = bias_rows(ends, n_seq, i, keys)

        def one(h):
            s = mm_nt(kk[0:keys, :], qm[h, i * TILE : (i + 1) * TILE, :]) + bias[0:keys, :]
            top = jnp.max(s, axis=0, keepdims=True)
            e = jnp.exp(s - top)
            total = jnp.sum(e, axis=0, keepdims=True)
            lse[h, 0:1, i * TILE : (i + 1) * TILE] = top + jnp.log(total)
            return mm(v_t[:, 0:keys], (e * (1.0 / total)).astype(BF))

        for pr in range(pairs):
            both = jnp.concatenate([one(2 * pr), one(2 * pr + 1)], axis=0)
            att_s[i * TILE : (i + 1) * TILE, pr * 128 : (pr + 1) * 128] = jnp.transpose(
                both
            ).astype(BF)

    def restore(i, _):
        src = pl.ds(pl.multiple_of(i * span, span), span)
        att[pl.ds(pl.multiple_of(offs[i], span), span), :] = att_s[src, :]
        return 0

    lax.fori_loop(0, n_span, restore, 0)


def attention(offs, ends, qkv, cos, sin, span, heads):
    rows = qkv.shape[0]
    return pl.pallas_call(
        functools.partial(attention_body, span, heads, ends.shape[0]),
        in_specs=[SMEM, SMEM, VMEM, VMEM, VMEM],
        out_specs=[VMEM] * 5,
        out_shape=[
            jax.ShapeDtypeStruct((rows, heads * HEAD), BF),
            jax.ShapeDtypeStruct((heads, rows, 128), BF),
            jax.ShapeDtypeStruct((rows, 128), BF),
            jax.ShapeDtypeStruct((rows, 128), BF),
            jax.ShapeDtypeStruct((heads, 1, rows), F32),
        ],
        scratch_shapes=[
            pltpu.VMEM((HEAD, rows), BF),
            pltpu.VMEM((rows, heads * HEAD), BF),
            pltpu.VMEM((rows, TILE), F32),
        ],
        compiler_params=params(40),
        cost_estimate=cost(3 * heads * rows * rows * 128, 8 << 20, heads * rows * rows),
        name="attention",
    )(offs, ends, qkv, cos, sin)


def attention_back_body(
    span, heads, n_seq, offs, ends, grad, qm, kk, vv, lse, cos, sin, out,
    agm, k_t, dq_s, dkk, dvv, bias,
):
    rows = grad.shape[0]
    n_span = rows // span
    pairs = heads // 2
    q_cols = heads * HEAD

    def prepare(i, _):
        src = pl.ds(pl.multiple_of(offs[i], span), span)
        dst = pl.ds(pl.multiple_of(i * span, span), span)
        low = lax.broadcasted_iota(jnp.int32, (span, 128), 1) < HEAD
        for pr in range(pairs):
            x = grad[src, pr * 128 : (pr + 1) * 128].astype(F32)
            agm[2 * pr, dst, :] = jnp.where(low, x, 0.0).astype(BF)
            agm[2 * pr + 1, dst, :] = jnp.where(low, 0.0, x).astype(BF)
        return 0

    lax.fori_loop(0, n_span, prepare, 0)
    k_t[...] = jnp.transpose(kk[...].astype(F32))[0:HEAD, :].astype(BF)
    dkk[...] = jnp.zeros_like(dkk)
    dvv[...] = jnp.zeros_like(dvv)
    for i in range(rows // TILE):
        keys = (i + 1) * TILE
        here = slice(i * TILE, (i + 1) * TILE)
        bias[0:keys, :] = bias_rows(ends, n_seq, i, keys)

        def one(h):
            q = qm[h, here, :]
            a = agm[h, here, :]
            s = mm_nt(kk[0:keys, :], q) + bias[0:keys, :]
            prob = jnp.exp(s - lse[h, 0:1, here])
            pg = mm_nt(vv[0:keys, :], a)
            delta = jnp.sum(prob * pg, axis=0, keepdims=True)
            ds = (prob * (pg - delta)).astype(BF)
            dkk[0:keys, :] += mm(ds, q)
            dvv[0:keys, :] += mm(prob.astype(BF), a)
            return mm(k_t[:, 0:keys], ds)

        for pr in range(pairs):
            both = jnp.concatenate([one(2 * pr), one(2 * pr + 1)], axis=0)
            dq_s[here, pr * 128 : (pr + 1) * 128] = jnp.transpose(both) * (1.0 / math.sqrt(HEAD))

    def restore(i, _):
        src = pl.ds(pl.multiple_of(i * span, span), span)
        dst = pl.ds(pl.multiple_of(offs[i], span), span)
        c, s = cos[dst, :], sin[dst, :]
        low = lax.broadcasted_iota(jnp.int32, (span, 128), 1) < HEAD
        for pr in range(pairs):
            x = dq_s[src, pr * 128 : (pr + 1) * 128]
            out[dst, pr * 128 : (pr + 1) * 128] = (x * c - half_swap(x) * s).astype(BF)
        k = dkk[src, :]
        v = dvv[src, :]
        x = jnp.where(low, k + pltpu.roll(k, HEAD, 1), v + pltpu.roll(v, HEAD, 1))
        x = x * jnp.where(low, c, 1.0) - half_swap(x) * jnp.where(low, s, 0.0)
        out[dst, q_cols : q_cols + 128] = x.astype(BF)
        return 0

    lax.fori_loop(0, n_span, restore, 0)


def attention_back(offs, ends, grad, qm, kk, vv, lse, cos, sin, span, heads):
    rows = grad.shape[0]
    return pl.pallas_call(
        functools.partial(attention_back_body, span, heads, ends.shape[0]),
        in_specs=[SMEM, SMEM] + [VMEM] * 7,
        out_specs=VMEM,
        out_shape=jax.ShapeDtypeStruct((rows, heads * HEAD + 128), BF),
        scratch_shapes=[
            pltpu.VMEM((heads, rows, 128), BF),
            pltpu.VMEM((HEAD, rows), BF),
            pltpu.VMEM((rows, heads * HEAD), F32),
            pltpu.VMEM((rows, 128), F32),
            pltpu.VMEM((rows, 128), F32),
            pltpu.VMEM((rows, TILE), F32),
        ],
        compiler_params=params(48),
        cost_estimate=cost(8 * heads * rows * rows * 128, 8 << 20, heads * rows * rows),
        name="attention_back",
    )(offs, ends, grad, qm, kk, vv, lse, cos, sin)


def out_norm_body(nz, n_f, ids, *refs):
    atts = refs[: 2 * nz]
    ws = refs[2 * nz : 2 * nz + 2 * n_f]
    xs = refs[2 * nz + 2 * n_f : 4 * nz + 2 * n_f]
    gain, hidden, normed, left, w_all, sems = refs[4 * nz + 2 * n_f :]
    z, f = ids[0], ids[1]
    cols = atts[0].shape[1]
    tok = xs[0].shape[0]
    copies = []
    for q in range(2):
        for k in range(n_f):
            copies.append(
                (ws[q * n_f + k], w_all.at[q, pl.ds(pl.multiple_of((f ^ k) * cols, 128), cols)])
            )
    for q in range(2):
        for k in range(nz):
            lanes = pl.ds(pl.multiple_of((z ^ k) * cols, 128), cols)
            for b in range(2 * nz):
                src = ((b // nz) ^ q) * nz + ((b % nz) ^ k)
                copies.append(
                    (
                        atts[q * nz + k].at[pl.ds(src * tok, tok)],
                        left.at[q, pl.ds(b * tok, tok), lanes],
                    )
                )
    copies = [
        pltpu.make_async_copy(src, dst, sems.at[i]) for i, (src, dst) in enumerate(copies)
    ]
    for copy in copies:
        copy.start()
    for copy in copies:
        copy.wait()
    per = TILE // tok
    g = gain[...]
    for b in range(2 * nz // per):
        at = slice(b * TILE, (b + 1) * TILE)
        acc = mm(left[0, at, :], w_all[0]) + mm(left[1, at, :], w_all[1])
        for j in range(per):
            h = acc[j * tok : (j + 1) * tok, :] + xs[b * per + j][...].astype(F32)
            if b == 0 and j == 0:
                hidden[...] = h
            r = lax.rsqrt(jnp.mean(h * h, axis=-1, keepdims=True) + EPS)
            lo = b * TILE + j * tok
            normed[lo : lo + tok, :] = (h * r * g).astype(BF)


def out_norm(ids, atts, ws, xs, gain, nz, n_f):
    rows, cols = atts[0].shape
    tok, width = xs[0].shape
    return pl.pallas_call(
        functools.partial(out_norm_body, nz, n_f),
        in_specs=[SMEM] + [ANY] * (2 * nz + 2 * n_f) + [VMEM] * (2 * nz + 1),
        out_specs=[VMEM] * 3,
        out_shape=[
            jax.ShapeDtypeStruct((tok, width), F32),
            jax.ShapeDtypeStruct((rows, width), BF),
            jax.ShapeDtypeStruct((2, rows, nz * cols), BF),
        ],
        scratch_shapes=[
            pltpu.VMEM((2, n_f * cols, width), BF),
            pltpu.SemaphoreType.DMA((4 * nz * nz + 2 * n_f,)),
        ],
        compiler_params=params(56),
        cost_estimate=cost(2 * rows * width * width, 20 << 20),
        name="out_norm",
    )(ids, *atts, *ws, *xs, gain)


def ffn_body(half, normed, cot, w_gu, wd, act, gg, ug, far, near):
    n_f, _, depth, _ = w_gu.shape
    i = pl.program_id(0)
    x = normed[...]
    gate = mm(x[:, 0:depth], w_gu[0, 0])
    up = mm(x[:, 0:depth], w_gu[0, 1])
    for k in range(1, n_f):
        piece = x[:, k * depth : (k + 1) * depth]
        gate = gate + mm(piece, w_gu[k, 0])
        up = up + mm(piece, w_gu[k, 1])
    grad = mm_nt(cot[...], wd[...])
    sig = 1.0 / (1.0 + jnp.exp(-gate))
    silu = gate * sig
    act[...] = (silu * up).astype(BF)
    g = (grad * up * sig * (1.0 + gate * (1.0 - sig))).astype(BF)
    u = (grad * silu).astype(BF)
    gg[...] = g
    ug[...] = u

    def emit(out):
        for k in range(n_f):
            out[:, k * depth : (k + 1) * depth] = (
                mm_nt(g, w_gu[k, 0]) + mm_nt(u, w_gu[k, 1])
            ).astype(BF)

    @pl.when(i < half)
    def _():
        emit(far)

    @pl.when(i >= half)
    def _():
        emit(near)


def ffn(normed, cot, w_gu, wd):
    rows, width = normed.shape
    ff_p = wd.shape[0]
    count = rows // TILE
    half = count // 2

    def turn(i):
        return (lax.rem(i + half, count), 0)

    tile_in = pl.BlockSpec((TILE, width), turn)
    tile_ff = pl.BlockSpec((TILE, ff_p), turn)
    return pl.pallas_call(
        functools.partial(ffn_body, half),
        grid=(count,),
        in_specs=[tile_in, tile_in, VMEM, VMEM],
        out_specs=[tile_ff, tile_ff, tile_ff]
        + [
            pl.BlockSpec((TILE, width), lambda i: (jnp.minimum(i, half - 1), 0)),
            pl.BlockSpec((TILE, width), lambda i: (jnp.maximum(i - half, 0), 0)),
        ],
        out_shape=[jax.ShapeDtypeStruct((rows, ff_p), BF)] * 3
        + [jax.ShapeDtypeStruct((rows // 2, width), BF)] * 2,
        compiler_params=params(48),
        cost_estimate=cost(10 * rows * width * ff_p, 20 << 20),
        name="ffn",
    )(normed, cot, w_gu, wd)


def terms_body(n_f, left, *refs):
    rights, out = refs[:-1], refs[-1]
    lt = left[...]
    rows_b = lt.shape[1] // n_f
    for j, right in enumerate(rights):
        total = mm_tn(lt, right[...]).astype(BF)
        for k in range(n_f):
            out[k, 0, j * rows_b : (j + 1) * rows_b, :] = total[k * rows_b : (k + 1) * rows_b, :]


def terms(left, rights, n_ctx, n_f):
    stacked = left.ndim == 3
    rows = left.shape[-2]
    width = left.size // rows
    cols = rights[0].shape[1]
    lanes = width // n_ctx
    deep = len(rights) * lanes // n_f
    if stacked:
        per = n_ctx // 2
        spec = pl.BlockSpec((None, rows, lanes), lambda i: (i // per, 0, lax.rem(i, per)))
    else:
        spec = pl.BlockSpec((rows, lanes), lambda i: (0, i))
    return pl.pallas_call(
        functools.partial(terms_body, n_f),
        grid=(n_ctx,),
        in_specs=[spec] + [VMEM] * len(rights),
        out_specs=pl.BlockSpec((n_f, 1, deep, cols), lambda i: (0, i, 0, 0)),
        out_shape=jax.ShapeDtypeStruct((n_f, n_ctx, deep, cols), BF),
        compiler_params=params(40),
        cost_estimate=cost(2 * rows * width * cols * len(rights), 16 << 20),
        name="terms",
    )(left, *rights)


def assemble_body(n_f, ff_b, recv, gate, up):
    n_ctx, both_rows, ff_p = recv.shape
    rows = both_rows // 2
    step = ff_p // n_f
    for c in range(n_ctx):
        for k in range(n_f):
            at = (k * n_ctx + c) * ff_b
            gate[:, at : at + ff_b] = recv[c, 0:rows, k * step : k * step + ff_b].astype(F32)
            up[:, at : at + ff_b] = recv[c, rows:both_rows, k * step : k * step + ff_b].astype(F32)


def assemble(recv, n_f, ff_b):
    n_ctx, both_rows, _ = recv.shape
    return pl.pallas_call(
        functools.partial(assemble_body, n_f, ff_b),
        in_specs=[VMEM],
        out_specs=[VMEM] * 2,
        out_shape=[jax.ShapeDtypeStruct((both_rows // 2, n_ctx * n_f * ff_b), F32)] * 2,
        compiler_params=params(24),
        cost_estimate=cost(0, 6 << 20),
        name="assemble",
    )(recv)


def after(value, *others):
    return lax.optimization_barrier((value,) + others)[0]


def make_body(n_ctx, n_fsdp):
    nz = n_ctx // 2
    both = ("ctx", "fsdp")
    core_swap = [(i, i ^ 1) for i in range(n_ctx)]

    def swap(x):
        return lax.ppermute(x, "ctx", core_swap)

    def chip(x, k):
        return lax.ppermute(x, "ctx", [(i, i ^ (2 * k)) for i in range(n_ctx)])

    def face(x, k):
        return lax.ppermute(x, "fsdp", [(i, i ^ k) for i in range(n_fsdp)])

    def pairs(links):
        return [(2 * a + core, 2 * b + core) for a, b in links for core in (0, 1)]

    def gather_ctx(x):
        if nz == 4:
            two = chip(x, 2)
            near = lax.ppermute(x, "ctx", pairs([(1, 2), (2, 1)]))
            one = chip(x, 1)
            relay = lax.ppermute(two, "ctx", pairs([(2, 3), (1, 0)]))
            z = lax.axis_index("ctx") // 2
            three = jnp.where((z == 1) | (z == 2), near, relay)
            mine = [x, one, two, three]
        else:
            mine = [x] + [chip(x, k) for k in range(1, nz)]
        return mine + [swap(m) for m in mine]

    def reduce_ctx(far, near):
        rows = near.shape[0] // nz
        other = swap(far)
        sums = [
            near[k * rows : (k + 1) * rows].astype(F32)
            + other[k * rows : (k + 1) * rows].astype(F32)
            for k in range(nz)
        ]
        low = [v.astype(BF) for v in sums]
        if nz == 4:
            far_end = lax.ppermute(low[3], "ctx", pairs([(0, 1), (3, 2)]))
            one = chip(low[1], 1)
            middle = lax.ppermute(low[3], "ctx", pairs([(1, 2), (2, 1)]))
            two = chip((sums[2] + far_end.astype(F32)).astype(BF), 2)
            parts = [one, middle, two]
        else:
            parts = [chip(low[k], k) for k in range(1, nz)]
        total = sums[0]
        for part in parts:
            total = total + part.astype(F32)
        return total

    def reduce_face(e):
        f = lax.axis_index("fsdp")
        total = lax.dynamic_index_in_dim(e, f, 0, keepdims=False).astype(F32)
        for k in range(1, n_fsdp):
            part = face(lax.dynamic_index_in_dim(e, f ^ k, 0, keepdims=False), k)
            total = total + part.astype(F32)
        return total

    def body(
        tokens,
        cotangent,
        lengths,
        span_order,
        gain_attn,
        w_query,
        w_key,
        w_value,
        w_out,
        gain_ffn,
        w_gate,
        w_up,
        w_down,
    ):
        c = lax.axis_index("ctx")
        f = lax.axis_index("fsdp")
        z = c // 2
        p = c % 2
        tok = tokens.shape[1]
        span = tok // 2
        width = tokens.shape[2]
        rows_all = n_ctx * tok
        q_cols = HEADS * HEAD // n_ctx
        heads = HEADS // n_ctx
        kv = c * KV_HEADS // n_ctx
        ff = w_gate.shape[1]
        ff_c = ff // n_ctx
        ff_b = ff_c // n_fsdp
        ff_p = -(-ff_c // 128) * 128
        ff_bp = ff_p // n_fsdp
        shard = w_query.shape[0]
        rows_b = width // (n_ctx * n_fsdp)

        spans = jnp.arange(span_order.shape[1], dtype=jnp.int32)
        dealt = jnp.sum(
            jnp.where(span_order[0][None, :] == spans[:, None], spans[None, :], 0), axis=1
        )
        dev = dealt // 2
        offs = ((((dev % 2) ^ p) * nz + ((dev // 2) ^ z)) * 2 + dealt % 2) * span
        offs = offs.astype(jnp.int32)
        ends = jnp.cumsum(lengths[0]).astype(jnp.int32)
        starts = ends - lengths[0]
        row = jnp.arange(rows_all, dtype=jnp.int32)
        block = row // tok
        slot = (((block % nz) ^ z) * 2 + (p ^ (block // nz))) * 2 + (row % tok) // span
        chosen = jnp.sum(
            jnp.where(slot[:, None] == spans[None, :], span_order[0][None, :], 0), axis=1
        )
        anchor = chosen * span + row % span
        segment = jnp.sum((anchor[:, None] >= ends[None, :]).astype(jnp.int32), axis=1)
        first = jnp.sum(
            jnp.where(
                segment[:, None] == jnp.arange(ends.shape[0], dtype=jnp.int32)[None, :],
                starts[None, :],
                0,
            ),
            axis=1,
        )
        pos = (anchor - first).astype(F32)
        lane = jnp.arange(128, dtype=jnp.int32)
        inverse = THETA ** (-((lane % (HEAD // 2)).astype(F32) * 2.0 / HEAD))
        angles = pos[:, None] * inverse[None, :]
        sign = jnp.where(lane % HEAD < HEAD // 2, -1.0, 1.0).astype(F32)
        cos = jnp.cos(angles)
        sin = jnp.sin(angles) * sign[None, :]

        x_own = tokens[0]
        xs = gather_ctx(x_own)

        def cols(w, start, size):
            return lax.dynamic_slice_in_dim(w, start, size, 1)

        chunks = shard // 128
        gains = jnp.concatenate(
            [gain_attn.reshape(chunks, 128), gain_ffn.reshape(chunks, 128)], axis=1
        )
        gains = jnp.pad(gains, ((0, 16 - chunks), (0, q_cols + 128 - 256)))
        pack = jnp.concatenate(
            [
                jnp.concatenate(
                    [
                        cols(w_query, c * q_cols, q_cols),
                        cols(w_key, kv * HEAD, HEAD),
                        cols(w_value, kv * HEAD, HEAD),
                    ],
                    1,
                ),
                gains,
            ],
            0,
        )
        packs = [pack] + [face(pack, k) for k in range(1, n_fsdp)]

        w_gate, w_up, w_down = lax.optimization_barrier((w_gate, w_up, w_down, xs[nz]))[:3]

        def slices(w):
            gap = jnp.zeros((shard, ff_bp - ff_b), BF)
            out = []
            for k in range(n_fsdp):
                out += [cols(w, k * (ff // n_fsdp) + c * ff_b, ff_b), gap]
            return jnp.concatenate(out, 1)

        w_gu = lax.all_gather(jnp.stack([slices(w_gate), slices(w_up)], 0), "fsdp", axis=0)
        wd_own = lax.dynamic_slice_in_dim(w_down, c * ff_b, ff_b, 0)
        wd = lax.all_gather(
            jnp.pad(wd_own, ((0, ff_bp - ff_b), (0, 0))), "fsdp", axis=0, tiled=True
        )
        wo_own = lax.dynamic_slice_in_dim(w_out, p * q_cols, q_cols, 0)
        wo_own = after(wo_own, *packs[1:])
        wo_mine = [wo_own] + [face(wo_own, k) for k in range(1, n_fsdp)]
        wos = wo_mine + [swap(w) for w in wo_mine]

        f_id = f.reshape(1).astype(jnp.int32)
        n1_all, qkv, wqkv, gains_all = norm_qkv(f_id, xs, packs, shard)
        gain1 = gains_all[:, :chunks, 0:128].reshape(width).astype(F32)
        gain2 = gains_all[:, :chunks, 128:256].reshape(width).astype(F32)

        cot_own = after(cotangent[0], *xs)
        cot = jnp.concatenate(gather_ctx(cot_own), 0)

        att, qm, kk, vv, lse = attention(offs, ends, qkv, cos, sin, span, heads)
        atts = gather_ctx(after(att, cot))
        ids = jnp.stack([z, f]).astype(jnp.int32)
        hidden, n2_all, att_all = out_norm(ids, atts, wos, xs, gain2[None, :], nz, n_fsdp)
        act, gg, ug, far, near = ffn(n2_all, cot, w_gu, wd)
        n2_grad = reduce_ctx(far, near)

        half = rows_all // 2
        e_gu = terms(n2_all, [gg, ug], n_ctx, n_fsdp)
        e_down = mm_tn(act, cot, BF)
        out_far = mm(act[half:], wd).astype(BF)
        out_near = mm(act[:half], wd).astype(BF)
        n2_grad = after(n2_grad, e_gu, e_down, out_far, out_near)
        e_gu = lax.psum_scatter(e_gu, "fsdp", scatter_dimension=0, tiled=False)
        e_down = lax.psum_scatter(e_down, "fsdp", scatter_dimension=0, tiled=True)

        r2 = lax.rsqrt(jnp.mean(hidden * hidden, axis=-1, keepdims=True) + EPS)
        weighted = n2_grad * gain2[None, :]
        hidden_grad = (
            cotangent[0].astype(F32)
            + r2 * weighted
            - hidden * (r2 * r2 * r2 * jnp.mean(weighted * hidden, axis=-1, keepdims=True))
        )
        branch = hidden_grad.astype(BF)
        pair_branch = jnp.concatenate([branch, swap(branch)], 0)
        wo_rel = jnp.concatenate(wo_mine, 0)
        agrads = mm_nt(pair_branch, wo_rel).astype(BF)
        def block_of(k):
            return cols(agrads, ((z ^ k) ^ f) * q_cols, q_cols)

        got = [block_of(0)] + [chip(block_of(k), k) for k in range(1, nz)]
        agrad = jnp.concatenate([g[:tok] for g in got] + [g[tok:] for g in got], 0)

        pair_late = after(pair_branch, agrad)

        def columns_of(k):
            return cols(pair_late, ((z ^ k) * 2 + p) * q_cols, q_cols)

        sent = [columns_of(0)] + [chip(columns_of(k), k) for k in range(1, nz)]
        branch_cols = jnp.concatenate([g[:tok] for g in sent] + [g[tok:] for g in sent], 0)

        dqkv = attention_back(offs, ends, agrad, qm, kk, vv, lse, cos, sin, span, heads)
        n1_far = mm_nt(dqkv[half:], wqkv).astype(BF)
        n1_near = mm_nt(dqkv[:half], wqkv).astype(BF)
        n1_grad = reduce_ctx(n1_far, n1_near)
        inputs = x_own.astype(F32)
        r1 = lax.rsqrt(jnp.mean(inputs * inputs, axis=-1, keepdims=True) + EPS)
        weighted = n1_grad * gain1[None, :]
        grad_in = (
            hidden_grad
            + r1 * weighted
            - inputs * (r1 * r1 * r1 * jnp.mean(weighted * inputs, axis=-1, keepdims=True))
        ).astype(BF)

        moves = []
        for ci in range(n_ctx):
            for fi in range(n_fsdp):
                moves.append((ci * n_fsdp + fi, fi * n_ctx + ci))
        grad_down = lax.ppermute(e_down[:ff_b], both, moves).astype(F32)
        out_far = after(out_far, agrad)
        output = (hidden + reduce_ctx(out_far, out_near)).astype(BF)
        e_out = reduce_face(terms(att_all, [branch_cols], n_ctx, n_fsdp))
        e_qkv = reduce_face(terms(n1_all, [dqkv], n_ctx, n_fsdp))

        def split(v):
            high = lax.reduce_precision(v, 8, 7)
            return high.astype(BF), (v - high).astype(BF)

        def row_sums(e, w_rows):
            return split(
                jnp.sum(e.astype(F32) * w_rows.astype(F32), axis=-1, keepdims=True)
            )

        per = n_ctx // n_fsdp
        mine_gu = w_gu.reshape(n_fsdp, 2, per, n_fsdp, rows_b, ff_p)
        mine_gu = lax.dynamic_index_in_dim(mine_gu, f, 3, keepdims=False)
        mine_gu = mine_gu.transpose(0, 2, 1, 3, 4).reshape(n_ctx, 2 * rows_b, ff_p)
        high, low = row_sums(e_gu, mine_gu)
        spot = jnp.arange(ff_p, dtype=jnp.int32)[None, None, :]
        ship = jnp.where(spot == ff_b, high, jnp.where(spot == ff_b + 1, low, e_gu))
        recv_gu = lax.all_to_all(ship, "ctx", 0, 0, tiled=True)

        mine_qkv = wqkv.reshape(n_ctx, n_fsdp, rows_b, q_cols + 128)
        mine_qkv = lax.dynamic_index_in_dim(mine_qkv, f, 1, keepdims=False)
        high, low = row_sums(e_qkv, mine_qkv)
        gap = jnp.zeros((n_ctx, rows_b, 126), BF)
        order = jnp.arange(n_ctx, dtype=jnp.int32)
        e_out = jnp.take(e_out.astype(BF), ((order % 2) ^ p) * nz + order // 2, axis=0)
        ship = jnp.concatenate([e_qkv.astype(BF), high, low, gap, e_out], -1)
        recv_qkv = lax.all_to_all(ship, "ctx", 0, 0, tiled=True).astype(F32)
        my_row = (c * n_fsdp + f) * rows_b
        gain1_r = lax.dynamic_slice_in_dim(gain1, my_row, rows_b, 0)
        gain2_r = lax.dynamic_slice_in_dim(gain2, my_row, rows_b, 0)

        grad_gate, grad_up = assemble(recv_gu, n_fsdp, ff_b)
        sum_gu = jnp.sum(recv_gu[:, :, ff_b : ff_b + 2].astype(F32), (0, 2))
        grad_g2 = (sum_gu[:rows_b] + sum_gu[rows_b:]) / gain2_r
        grad_out = recv_qkv[:, :, q_cols + 256 :].transpose(1, 0, 2).reshape(rows_b, -1)
        grad_query = recv_qkv[:, :, :q_cols].transpose(1, 0, 2).reshape(rows_b, -1)
        share = n_ctx // KV_HEADS

        def lay_kv(start):
            part = recv_qkv[:, :, start : start + HEAD].reshape(KV_HEADS, share, rows_b, HEAD)
            return jnp.sum(part, 1).transpose(1, 0, 2).reshape(rows_b, -1)

        grad_key = lay_kv(q_cols)
        grad_value = lay_kv(q_cols + HEAD)
        grad_g1 = jnp.sum(recv_qkv[:, :, q_cols + 128 : q_cols + 130], (0, 2)) / gain1_r
        return (
            output[None],
            grad_in[None],
            grad_g1,
            grad_query,
            grad_key,
            grad_value,
            grad_out,
            grad_g2,
            grad_gate,
            grad_up,
            grad_down,
        )

    return body


def solution(mesh):
    body = make_body(mesh.shape["ctx"], mesh.shape["fsdp"])
    both = ("ctx", "fsdp")
    in_specs = (
        P("fsdp", "ctx", None),
        P("fsdp", "ctx", None),
        P("fsdp", None),
        P("fsdp", None),
        P("fsdp"),
        P("fsdp", None),
        P("fsdp", None),
        P("fsdp", None),
        P("fsdp", None),
        P("fsdp"),
        P("fsdp", None),
        P("fsdp", None),
        P("fsdp", None),
    )
    out_specs = (
        P("fsdp", "ctx", None),
        P("fsdp", "ctx", None),
        P(both),
        P(both, None),
        P(both, None),
        P(both, None),
        P(both, None),
        P(both),
        P(both, None),
        P(both, None),
        P(both, None),
    )
    return jax.shard_map(body, mesh=mesh, in_specs=in_specs, out_specs=out_specs, check_vma=False)
```

```python
import functools
import math

import jax
import jax.numpy as jnp
from jax import lax
from jax.experimental import pallas as pl
from jax.experimental.pallas import tpu as pltpu
from jax.sharding import PartitionSpec as P


HEADS = 32
KV_HEADS = 4
HEAD = 64
EPS = 1e-05
THETA = 10000.0
NEGATIVE = -1e30
BF = jnp.bfloat16
F32 = jnp.float32
TILE = 256
VMEM = pl.BlockSpec(memory_space=pltpu.VMEM)
SMEM = pl.BlockSpec(memory_space=pltpu.SMEM)
ANY = pl.BlockSpec(memory_space=pl.ANY)


def dot(left, right, dims, out=F32):
    return lax.dot_general(left, right, (dims, ((), ())), preferred_element_type=out)


def mm(left, right, out=F32):
    return dot(left, right, ((1,), (0,)), out)


def mm_nt(left, right, out=F32):
    return dot(left, right, ((1,), (1,)), out)


def mm_tn(left, right, out=F32):
    return dot(left, right, ((0,), (0,)), out)


def params(mb):
    return pltpu.CompilerParams(vmem_limit_bytes=mb << 20)


def cost(flops, moved, trans=0):
    return pl.CostEstimate(flops=int(flops), bytes_accessed=int(moved), transcendentals=int(trans))


def norm_qkv_body(n_x, n_f, shard, ids, *refs):
    xs = refs[:n_x]
    packs = refs[n_x : n_x + n_f]
    normed, qkv, w_all, gains, row, sems = refs[n_x + n_f :]
    me = ids[0]
    copies = []
    for k in range(n_f):
        at = me ^ k
        copies.append(
            pltpu.make_async_copy(
                packs[k].at[pl.ds(0, shard)],
                w_all.at[pl.ds(pl.multiple_of(at * shard, shard), shard)],
                sems.at[k],
            )
        )
        copies.append(
            pltpu.make_async_copy(packs[k].at[pl.ds(shard, 16)], gains.at[at], sems.at[n_f + k])
        )
    for copy in copies:
        copy.start()
    for copy in copies:
        copy.wait()
    for g in range(n_f):
        part = gains[g].astype(F32)
        for j in range(shard // 128):
            start = g * shard + j * 128
            row[0:1, start : start + 128] = part[j : j + 1, 0:128]
    tok = xs[0].shape[0]
    gain = row[...]
    for b in range(n_x):
        x = xs[b][...].astype(F32)
        r = lax.rsqrt(jnp.mean(x * x, axis=-1, keepdims=True) + EPS)
        normed[b * tok : (b + 1) * tok, :] = (x * r * gain).astype(BF)
    qkv[...] = mm(normed[...], w_all[...])


def norm_qkv(f_id, xs, packs, shard):
    n_x, n_f = len(xs), len(packs)
    tok, width = xs[0].shape
    cols = packs[0].shape[1]
    rows = n_x * tok
    return pl.pallas_call(
        functools.partial(norm_qkv_body, n_x, n_f, shard),
        in_specs=[SMEM] + [VMEM] * n_x + [ANY] * n_f,
        out_specs=[VMEM] * 4,
        out_shape=[
            jax.ShapeDtypeStruct((rows, width), BF),
            jax.ShapeDtypeStruct((rows, cols), F32),
            jax.ShapeDtypeStruct((width, cols), BF),
            jax.ShapeDtypeStruct((n_f, 16, cols), BF),
        ],
        scratch_shapes=[pltpu.VMEM((1, width), F32), pltpu.SemaphoreType.DMA((2 * n_f,))],
        compiler_params=params(40),
        cost_estimate=cost(2 * rows * width * cols, 4 * rows * width),
        name="norm_qkv",
    )(f_id, *xs, *packs)


def half_swap(x):
    lane = lax.broadcasted_iota(jnp.int32, x.shape, 1)
    return jnp.where(
        lane % HEAD < HEAD // 2, pltpu.roll(x, 128 - HEAD // 2, 1), pltpu.roll(x, HEAD // 2, 1)
    )


def bias_rows(ends, n_seq, i, keys):
    t = i * TILE + lax.broadcasted_iota(jnp.int32, (1, TILE), 1)
    first = jnp.zeros((1, TILE), jnp.int32)
    for s in range(n_seq):
        first = jnp.where(t >= ends[s], ends[s], first)
    u = lax.broadcasted_iota(jnp.int32, (keys, TILE), 0)
    return jnp.where((u <= t) & (u >= first), 0.0, NEGATIVE)


def attention_body(
    span, heads, n_seq, offs, ends, qkv, cos, sin, att, qm, kk, vv, lse, v_t, att_s, bias
):
    rows = qkv.shape[0]
    n_span = rows // span
    pairs = heads // 2
    q_cols = heads * HEAD

    def prepare(i, _):
        src = pl.ds(pl.multiple_of(offs[i], span), span)
        dst = pl.ds(pl.multiple_of(i * span, span), span)
        c, s = cos[src, :], sin[src, :]
        low = lax.broadcasted_iota(jnp.int32, (span, 128), 1) < HEAD
        for pr in range(pairs):
            x = qkv[src, pr * 128 : (pr + 1) * 128]
            q = (x * c + half_swap(x) * s).astype(BF).astype(F32) * (1.0 / math.sqrt(HEAD))
            qm[2 * pr, dst, :] = jnp.where(low, q, 0.0).astype(BF)
            qm[2 * pr + 1, dst, :] = jnp.where(low, 0.0, q).astype(BF)
        x = qkv[src, q_cols : q_cols + 128]
        kv = x * jnp.where(low, c, 1.0) + half_swap(x) * jnp.where(low, s, 0.0)
        other = pltpu.roll(kv, HEAD, 1)
        kk[dst, :] = jnp.where(low, kv, other).astype(BF)
        vv[dst, :] = jnp.where(low, other, kv).astype(BF)
        return 0

    lax.fori_loop(0, n_span, prepare, 0)
    v_t[...] = jnp.transpose(vv[...].astype(F32))[0:HEAD, :].astype(BF)
    for i in range(rows // TILE):
        keys = (i + 1) * TILE
        bias[0:keys, :] = bias_rows(ends, n_seq, i, keys)

        def one(h):
            s = mm_nt(kk[0:keys, :], qm[h, i * TILE : (i + 1) * TILE, :]) + bias[0:keys, :]
            top = jnp.max(s, axis=0, keepdims=True)
            e = jnp.exp(s - top)
            total = jnp.sum(e, axis=0, keepdims=True)
            lse[h, 0:1, i * TILE : (i + 1) * TILE] = top + jnp.log(total)
            return mm(v_t[:, 0:keys], (e * (1.0 / total)).astype(BF))

        for pr in range(pairs):
            both = jnp.concatenate([one(2 * pr), one(2 * pr + 1)], axis=0)
            att_s[i * TILE : (i + 1) * TILE, pr * 128 : (pr + 1) * 128] = jnp.transpose(
                both
            ).astype(BF)

    def restore(i, _):
        src = pl.ds(pl.multiple_of(i * span, span), span)
        att[pl.ds(pl.multiple_of(offs[i], span), span), :] = att_s[src, :]
        return 0

    lax.fori_loop(0, n_span, restore, 0)


def attention(offs, ends, qkv, cos, sin, span, heads):
    rows = qkv.shape[0]
    return pl.pallas_call(
        functools.partial(attention_body, span, heads, ends.shape[0]),
        in_specs=[SMEM, SMEM, VMEM, VMEM, VMEM],
        out_specs=[VMEM] * 5,
        out_shape=[
            jax.ShapeDtypeStruct((rows, heads * HEAD), BF),
            jax.ShapeDtypeStruct((heads, rows, 128), BF),
            jax.ShapeDtypeStruct((rows, 128), BF),
            jax.ShapeDtypeStruct((rows, 128), BF),
            jax.ShapeDtypeStruct((heads, 1, rows), F32),
        ],
        scratch_shapes=[
            pltpu.VMEM((HEAD, rows), BF),
            pltpu.VMEM((rows, heads * HEAD), BF),
            pltpu.VMEM((rows, TILE), F32),
        ],
        compiler_params=params(40),
        cost_estimate=cost(3 * heads * rows * rows * 128, 8 << 20, heads * rows * rows),
        name="attention",
    )(offs, ends, qkv, cos, sin)


def attention_back_body(
    span, heads, n_seq, n_piece, offs, ends, *refs
):
    pieces = refs[:n_piece]
    qm, kk, vv, lse, cos, sin, out, grad, agm, k_t, dq_s, dkk, dvv, bias = refs[n_piece:]
    rows = grad.shape[0]
    tok = pieces[0].shape[0] // 2
    for q in range(2):
        for k in range(n_piece):
            at = (q * n_piece + k) * tok
            grad[at : at + tok, :] = pieces[k][q * tok : (q + 1) * tok, :]
    n_span = rows // span
    pairs = heads // 2
    q_cols = heads * HEAD

    def prepare(i, _):
        src = pl.ds(pl.multiple_of(offs[i], span), span)
        dst = pl.ds(pl.multiple_of(i * span, span), span)
        low = lax.broadcasted_iota(jnp.int32, (span, 128), 1) < HEAD
        for pr in range(pairs):
            x = grad[src, pr * 128 : (pr + 1) * 128].astype(F32)
            agm[2 * pr, dst, :] = jnp.where(low, x, 0.0).astype(BF)
            agm[2 * pr + 1, dst, :] = jnp.where(low, 0.0, x).astype(BF)
        return 0

    lax.fori_loop(0, n_span, prepare, 0)
    k_t[...] = jnp.transpose(kk[...].astype(F32))[0:HEAD, :].astype(BF)
    dkk[...] = jnp.zeros_like(dkk)
    dvv[...] = jnp.zeros_like(dvv)
    for i in range(rows // TILE):
        keys = (i + 1) * TILE
        here = slice(i * TILE, (i + 1) * TILE)
        bias[0:keys, :] = bias_rows(ends, n_seq, i, keys)

        def one(h):
            q = qm[h, here, :]
            a = agm[h, here, :]
            s = mm_nt(kk[0:keys, :], q) + bias[0:keys, :]
            prob = jnp.exp(s - lse[h, 0:1, here])
            pg = mm_nt(vv[0:keys, :], a)
            delta = jnp.sum(prob * pg, axis=0, keepdims=True)
            ds = (prob * (pg - delta)).astype(BF)
            dkk[0:keys, :] += mm(ds, q)
            dvv[0:keys, :] += mm(prob.astype(BF), a)
            return mm(k_t[:, 0:keys], ds)

        for pr in range(pairs):
            both = jnp.concatenate([one(2 * pr), one(2 * pr + 1)], axis=0)
            dq_s[here, pr * 128 : (pr + 1) * 128] = jnp.transpose(both) * (1.0 / math.sqrt(HEAD))

    def restore(i, _):
        src = pl.ds(pl.multiple_of(i * span, span), span)
        dst = pl.ds(pl.multiple_of(offs[i], span), span)
        c, s = cos[dst, :], sin[dst, :]
        low = lax.broadcasted_iota(jnp.int32, (span, 128), 1) < HEAD
        for pr in range(pairs):
            x = dq_s[src, pr * 128 : (pr + 1) * 128]
            out[dst, pr * 128 : (pr + 1) * 128] = (x * c - half_swap(x) * s).astype(BF)
        k = dkk[src, :]
        v = dvv[src, :]
        x = jnp.where(low, k + pltpu.roll(k, HEAD, 1), v + pltpu.roll(v, HEAD, 1))
        x = x * jnp.where(low, c, 1.0) - half_swap(x) * jnp.where(low, s, 0.0)
        out[dst, q_cols : q_cols + 128] = x.astype(BF)
        return 0

    lax.fori_loop(0, n_span, restore, 0)


def attention_back(offs, ends, pieces, qm, kk, vv, lse, cos, sin, span, heads):
    rows = kk.shape[0]
    return pl.pallas_call(
        functools.partial(attention_back_body, span, heads, ends.shape[0], len(pieces)),
        in_specs=[SMEM, SMEM] + [VMEM] * (6 + len(pieces)),
        out_specs=VMEM,
        out_shape=jax.ShapeDtypeStruct((rows, heads * HEAD + 128), BF),
        scratch_shapes=[
            pltpu.VMEM((rows, heads * HEAD), BF),
            pltpu.VMEM((heads, rows, 128), BF),
            pltpu.VMEM((HEAD, rows), BF),
            pltpu.VMEM((rows, heads * HEAD), F32),
            pltpu.VMEM((rows, 128), F32),
            pltpu.VMEM((rows, 128), F32),
            pltpu.VMEM((rows, TILE), F32),
        ],
        compiler_params=params(48),
        cost_estimate=cost(8 * heads * rows * rows * 128, 8 << 20, heads * rows * rows),
        name="attention_back",
    )(offs, ends, *pieces, qm, kk, vv, lse, cos, sin)


def out_norm_body(nz, n_f, n_w, ids, *refs):
    atts = refs[: 2 * nz]
    ws = refs[2 * nz : 2 * nz + 2 * n_w]
    xs = refs[2 * nz + 2 * n_w : 4 * nz + 2 * n_w]
    gain, hidden, normed, left, w_all, sems = refs[4 * nz + 2 * n_w :]
    z, f = ids[0], ids[1]
    cols = atts[0].shape[1]
    tok = xs[0].shape[0]
    copies = []
    for q in range(2):
        used = 0
        for k in range(n_f):
            done = 0
            while done < cols:
                piece = ws[q * n_w + used]
                deep = piece.shape[0]
                at = pl.multiple_of((f ^ k) * cols + done, 64)
                copies.append((piece, w_all.at[q, pl.ds(at, deep)]))
                done += deep
                used += 1
    for q in range(2):
        for k in range(nz):
            lanes = pl.ds(pl.multiple_of((z ^ k) * cols, 128), cols)
            for b in range(2 * nz):
                src = ((b // nz) ^ q) * nz + ((b % nz) ^ k)
                copies.append(
                    (
                        atts[q * nz + k].at[pl.ds(src * tok, tok)],
                        left.at[q, pl.ds(b * tok, tok), lanes],
                    )
                )
    copies = [
        pltpu.make_async_copy(src, dst, sems.at[i]) for i, (src, dst) in enumerate(copies)
    ]
    for copy in copies:
        copy.start()
    for copy in copies:
        copy.wait()
    per = TILE // tok
    g = gain[...]
    for b in range(2 * nz // per):
        at = slice(b * TILE, (b + 1) * TILE)
        acc = mm(left[0, at, :], w_all[0]) + mm(left[1, at, :], w_all[1])
        for j in range(per):
            h = acc[j * tok : (j + 1) * tok, :] + xs[b * per + j][...].astype(F32)
            if b == 0 and j == 0:
                hidden[...] = h
            r = lax.rsqrt(jnp.mean(h * h, axis=-1, keepdims=True) + EPS)
            lo = b * TILE + j * tok
            normed[lo : lo + tok, :] = (h * r * g).astype(BF)


def out_norm(ids, atts, ws, xs, gain, nz, n_f):
    rows, cols = atts[0].shape
    tok, width = xs[0].shape
    return pl.pallas_call(
        functools.partial(out_norm_body, nz, n_f, len(ws) // 2),
        in_specs=[SMEM] + [ANY] * (2 * nz + len(ws)) + [VMEM] * (2 * nz + 1),
        out_specs=[VMEM] * 3,
        out_shape=[
            jax.ShapeDtypeStruct((tok, width), F32),
            jax.ShapeDtypeStruct((rows, width), BF),
            jax.ShapeDtypeStruct((2, rows, nz * cols), BF),
        ],
        scratch_shapes=[
            pltpu.VMEM((2, n_f * cols, width), BF),
            pltpu.SemaphoreType.DMA((4 * nz * nz + len(ws),)),
        ],
        compiler_params=params(56),
        cost_estimate=cost(2 * rows * width * width, 20 << 20),
        name="out_norm",
    )(ids, *atts, *ws, *xs, gain)


def ffn_body(half, n_f, n_w, n_held, ids, normed, cot, *refs):
    ws = refs[:n_w]
    wd = refs[n_w]
    act, gg, ug, far, near = refs[n_w + 1 + n_held :]
    f = ids[0]
    i = pl.program_id(0)
    gates = [w.at[0] for w in ws[:n_f]]
    ups = [w.at[1] for w in ws[: n_f - 1]]
    ups.append(ws[n_f - 1].at[1] if n_w == n_f else ws[n_f].at[0])
    depth = gates[0].shape[0]
    lanes = [pl.ds(pl.multiple_of((f ^ k) * depth, 128), depth) for k in range(n_f)]
    gate = mm(normed[:, lanes[0]], gates[0][...])
    up = mm(normed[:, lanes[0]], ups[0][...])
    for k in range(1, n_f):
        piece = normed[:, lanes[k]]
        gate = gate + mm(piece, gates[k][...])
        up = up + mm(piece, ups[k][...])
    grad = mm_nt(cot[...], wd[...])
    sig = 1.0 / (1.0 + jnp.exp(-gate))
    silu = gate * sig
    act[...] = (silu * up).astype(BF)
    g = (grad * up * sig * (1.0 + gate * (1.0 - sig))).astype(BF)
    u = (grad * silu).astype(BF)
    gg[...] = g
    ug[...] = u

    def emit(out):
        for k in range(n_f):
            out[:, lanes[k]] = (mm_nt(g, gates[k][...]) + mm_nt(u, ups[k][...])).astype(BF)

    @pl.when(i < half)
    def _():
        emit(far)

    @pl.when(i >= half)
    def _():
        emit(near)


def ffn(f_id, normed, cot, ws, wd, n_f, base, held):
    rows, width = normed.shape
    ff_p = wd.shape[0]
    count = rows // TILE // 2
    half = count // 2

    def turn(i):
        other = jnp.where(i < half, count, 0)
        return (other + base + lax.rem(i, half), 0)

    tile_in = pl.BlockSpec((TILE, width), turn)
    tile_ff = pl.BlockSpec((TILE, ff_p), turn)
    first_held = 4 + len(ws)
    return pl.pallas_call(
        functools.partial(ffn_body, half, n_f, len(ws), len(held)),
        grid=(count,),
        in_specs=[SMEM, tile_in, tile_in] + [VMEM] * (len(ws) + 1) + [ANY] * len(held),
        out_specs=[tile_ff, tile_ff, tile_ff]
        + [
            pl.BlockSpec((TILE, width), lambda i: (jnp.minimum(i, half - 1), 0)),
            pl.BlockSpec((TILE, width), lambda i: (jnp.maximum(i - half, 0), 0)),
        ],
        out_shape=[jax.ShapeDtypeStruct((rows, ff_p), BF)] * 3
        + [jax.ShapeDtypeStruct((rows // 4, width), BF)] * 2,
        input_output_aliases={first_held + j: j for j in range(len(held))},
        compiler_params=params(48),
        cost_estimate=cost(5 * rows * width * ff_p, 20 << 20),
        name="ffn",
    )(f_id, normed, cot, *ws, wd, *held)


def terms_body(n_f, joined, left, *refs):
    if joined:
        pieces, out, whole = refs[:-2], refs[-2], refs[-1]
        n_piece, tok = len(pieces), pieces[0].shape[0] // 2

        @pl.when(pl.program_id(0) == 0)
        def _():
            for q in range(2):
                for k in range(n_piece):
                    at = (q * n_piece + k) * tok
                    whole[at : at + tok, :] = pieces[k][q * tok : (q + 1) * tok, :]

        rights = [whole]
    else:
        rights, out = refs[:-1], refs[-1]
    lt = left[...]
    rows_b = lt.shape[1] // n_f
    for j, right in enumerate(rights):
        total = mm_tn(lt, right[...]).astype(BF)
        for k in range(n_f):
            out[k, 0, j * rows_b : (j + 1) * rows_b, :] = total[k * rows_b : (k + 1) * rows_b, :]


def terms(left, rights, n_ctx, n_f, joined=False):
    stacked = left.ndim == 3
    rows = left.shape[-2]
    width = left.size // rows
    cols = rights[0].shape[1]
    lanes = width // n_ctx
    deep = (1 if joined else len(rights)) * lanes // n_f
    if stacked:
        per = n_ctx // 2
        spec = pl.BlockSpec((None, rows, lanes), lambda i: (i // per, 0, lax.rem(i, per)))
    else:
        spec = pl.BlockSpec((rows, lanes), lambda i: (0, i))
    return pl.pallas_call(
        functools.partial(terms_body, n_f, joined),
        grid=(n_ctx,),
        scratch_shapes=[pltpu.VMEM((rows, cols), BF)] if joined else [],
        in_specs=[spec] + [VMEM] * len(rights),
        out_specs=pl.BlockSpec((n_f, 1, deep, cols), lambda i: (0, i, 0, 0)),
        out_shape=jax.ShapeDtypeStruct((n_f, n_ctx, deep, cols), BF),
        compiler_params=params(40),
        cost_estimate=cost(2 * rows * width * cols * len(rights), 16 << 20),
        name="terms",
    )(left, *rights)


def assemble_body(n_f, ff_b, recv, gate, up):
    n_ctx, both_rows, ff_p = recv.shape
    rows = both_rows // 2
    step = ff_p // n_f
    for c in range(n_ctx):
        for k in range(n_f):
            at = (k * n_ctx + c) * ff_b
            gate[:, at : at + ff_b] = recv[c, 0:rows, k * step : k * step + ff_b].astype(F32)
            up[:, at : at + ff_b] = recv[c, rows:both_rows, k * step : k * step + ff_b].astype(F32)


def assemble(recv, n_f, ff_b):
    n_ctx, both_rows, _ = recv.shape
    return pl.pallas_call(
        functools.partial(assemble_body, n_f, ff_b),
        in_specs=[VMEM],
        out_specs=[VMEM] * 2,
        out_shape=[jax.ShapeDtypeStruct((both_rows // 2, n_ctx * n_f * ff_b), F32)] * 2,
        compiler_params=params(24),
        cost_estimate=cost(0, 6 << 20),
        name="assemble",
    )(recv)


def after(value, *others):
    return lax.optimization_barrier((value,) + others)[0]


def make_body(n_ctx, n_fsdp):
    nz = n_ctx // 2
    both = ("ctx", "fsdp")
    core_swap = [(i, i ^ 1) for i in range(n_ctx)]

    def swap(x):
        return lax.ppermute(x, "ctx", core_swap)

    def chip(x, k):
        return lax.ppermute(x, "ctx", [(i, i ^ (2 * k)) for i in range(n_ctx)])

    def face(x, k):
        return lax.ppermute(x, "fsdp", [(i, i ^ k) for i in range(n_fsdp)])

    def pairs(links):
        return [(2 * a + core, 2 * b + core) for a, b in links for core in (0, 1)]

    def gather_ctx(x):
        if nz == 4:
            two = chip(x, 2)
            near = lax.ppermute(x, "ctx", pairs([(1, 2), (2, 1)]))
            one = chip(x, 1)
            relay = lax.ppermute(two, "ctx", pairs([(2, 3), (1, 0)]))
            z = lax.axis_index("ctx") // 2
            three = jnp.where((z == 1) | (z == 2), near, relay)
            mine = [x, one, two, three]
        else:
            mine = [x] + [chip(x, k) for k in range(1, nz)]
        return mine + [swap(m) for m in mine]

    def reduce_ctx(far, near, wait=None):
        rows = 2 * near[0].shape[0] // nz
        sums = []
        for part in (1, 0):
            other = swap(far[part])
            sums += [
                near[part][k * rows : (k + 1) * rows].astype(F32)
                + other[k * rows : (k + 1) * rows].astype(F32)
                for k in range(nz // 2)
            ]
        sums = sums[nz // 2 :] + sums[: nz // 2]
        low = [v.astype(BF) for v in sums]
        if wait is not None:
            low = [after(v, wait) for v in low]
        if nz == 4:
            far_end = lax.ppermute(low[3], "ctx", pairs([(0, 1), (3, 2)]))
            middle = lax.ppermute(low[3], "ctx", pairs([(1, 2), (2, 1)]))
            one = chip(low[1], 1)
            two = chip((low[2].astype(F32) + far_end.astype(F32)).astype(BF), 2)
            parts = [one, middle, two]
        else:
            parts = [chip(low[k], k) for k in range(1, nz)]
        total = sums[0]
        for part in parts:
            total = total + part.astype(F32)
        return total

    def gather_face(x):
        if n_fsdp != 4:
            return [x] + [face(x, k) for k in range(1, n_fsdp)]
        one, two = face(x, 1), face(x, 2)
        half = x.shape[0] // 2
        return [x, one, two, face(two[:half], 1), face(one[half:], 2)]

    def slot_of(e, i):
        return lax.dynamic_index_in_dim(e, i, 0, keepdims=False)

    def reduce_face(e, slot):
        total = slot_of(e, slot).astype(F32)
        parts = [face(slot_of(e, slot ^ k), k) for k in range(1, n_fsdp)]
        for part in parts:
            total = total + part.astype(F32)
        return total

    def reduce_square(e, slot, wait):
        if n_fsdp != 4:
            return reduce_face(e, slot)
        half = e.shape[1] // 2
        corner = slot_of(e, slot ^ 3)
        low = face(corner[:half], 1)
        high = face(corner[half:], 2)
        if wait is not None:
            low, high = after(low, wait), after(high, wait)
        two = slot_of(e, slot ^ 2)
        one = slot_of(e, slot ^ 1)
        two = jnp.concatenate(
            [(two[:half].astype(F32) + low.astype(F32)).astype(BF), two[half:]], 0
        )
        one = jnp.concatenate(
            [one[:half], (one[half:].astype(F32) + high.astype(F32)).astype(BF)], 0
        )
        parts = [face(one, 1), face(two, 2)]
        total = slot_of(e, slot).astype(F32)
        for part in parts:
            total = total + part.astype(F32)
        return total

    def body(
        tokens,
        cotangent,
        lengths,
        span_order,
        gain_attn,
        w_query,
        w_key,
        w_value,
        w_out,
        gain_ffn,
        w_gate,
        w_up,
        w_down,
    ):
        c = lax.axis_index("ctx")
        f = lax.axis_index("fsdp")
        z = c // 2
        p = c % 2
        tok = tokens.shape[1]
        span = tok // 2
        width = tokens.shape[2]
        rows_all = n_ctx * tok
        q_cols = HEADS * HEAD // n_ctx
        heads = HEADS // n_ctx
        kv = c * KV_HEADS // n_ctx
        ff = w_gate.shape[1]
        ff_c = ff // n_ctx
        ff_b = ff_c // n_fsdp
        ff_p = -(-ff_c // 128) * 128
        ff_bp = ff_p // n_fsdp
        shard = w_query.shape[0]
        rows_b = width // (n_ctx * n_fsdp)

        spans = jnp.arange(span_order.shape[1], dtype=jnp.int32)
        dealt = jnp.sum(
            jnp.where(span_order[0][None, :] == spans[:, None], spans[None, :], 0), axis=1
        )
        dev = dealt // 2
        offs = ((((dev % 2) ^ p) * nz + ((dev // 2) ^ z)) * 2 + dealt % 2) * span
        offs = offs.astype(jnp.int32)
        ends = jnp.cumsum(lengths[0]).astype(jnp.int32)
        starts = ends - lengths[0]
        row = jnp.arange(rows_all, dtype=jnp.int32)
        block = row // tok
        slot = (((block % nz) ^ z) * 2 + (p ^ (block // nz))) * 2 + (row % tok) // span
        chosen = jnp.sum(
            jnp.where(slot[:, None] == spans[None, :], span_order[0][None, :], 0), axis=1
        )
        anchor = chosen * span + row % span
        segment = jnp.sum((anchor[:, None] >= ends[None, :]).astype(jnp.int32), axis=1)
        first = jnp.sum(
            jnp.where(
                segment[:, None] == jnp.arange(ends.shape[0], dtype=jnp.int32)[None, :],
                starts[None, :],
                0,
            ),
            axis=1,
        )
        pos = (anchor - first).astype(F32)
        lane = jnp.arange(128, dtype=jnp.int32)
        inverse = THETA ** (-((lane % (HEAD // 2)).astype(F32) * 2.0 / HEAD))
        angles = pos[:, None] * inverse[None, :]
        sign = jnp.where(lane % HEAD < HEAD // 2, -1.0, 1.0).astype(F32)
        cos = jnp.cos(angles)
        sin = jnp.sin(angles) * sign[None, :]

        x_own = tokens[0]
        xs = gather_ctx(x_own)

        def cols(w, start, size):
            return lax.dynamic_slice_in_dim(w, start, size, 1)

        chunks = shard // 128
        gains = jnp.concatenate(
            [gain_attn.reshape(chunks, 128), gain_ffn.reshape(chunks, 128)], axis=1
        )
        gains = jnp.pad(gains, ((0, 16 - chunks), (0, q_cols + 128 - 256)))
        pack = jnp.concatenate(
            [
                jnp.concatenate(
                    [
                        cols(w_query, c * q_cols, q_cols),
                        cols(w_key, kv * HEAD, HEAD),
                        cols(w_value, kv * HEAD, HEAD),
                    ],
                    1,
                ),
                gains,
            ],
            0,
        )
        packs = [pack] + [face(pack, k) for k in range(1, n_fsdp)]
        wo_own = lax.dynamic_slice_in_dim(w_out, p * q_cols, q_cols, 0)
        wo_mine = gather_face(wo_own)

        def slices(w):
            gap = jnp.zeros((shard, ff_bp - ff_b), BF)
            out = []
            for k in range(n_fsdp):
                out += [cols(w, k * (ff // n_fsdp) + c * ff_b, ff_b), gap]
            return jnp.concatenate(out, 1)

        gu_own = jnp.stack([slices(w_gate), slices(w_up)], 0)
        w_gu = gather_face(gu_own)
        wd_own = jnp.pad(
            lax.dynamic_slice_in_dim(w_down, c * ff_b, ff_b, 0), ((0, ff_bp - ff_b), (0, 0))
        )
        wd_parts = gather_face(wd_own)
        wd = jnp.zeros((ff_p, width), BF)
        for k in range(n_fsdp):
            at = (f ^ k) * ff_bp
            wd = lax.dynamic_update_slice_in_dim(wd, wd_parts[k], at, 0)
        if len(wd_parts) > n_fsdp:
            at = (f ^ (n_fsdp - 1)) * ff_bp + ff_bp // 2
            wd = lax.dynamic_update_slice_in_dim(wd, wd_parts[n_fsdp], at, 0)
        wos = wo_mine + [swap(w) for w in wo_mine]

        f_id = f.reshape(1).astype(jnp.int32)
        n1_all, qkv, wqkv, gains_all = norm_qkv(f_id, xs, packs, shard)
        gain1 = gains_all[:, :chunks, 0:128].reshape(width).astype(F32)
        gain2 = gains_all[:, :chunks, 128:256].reshape(width).astype(F32)

        cot_own = after(cotangent[0], *xs[:nz])
        cot = jnp.concatenate(gather_ctx(cot_own), 0)

        att, qm, kk, vv, lse = attention(offs, ends, qkv, cos, sin, span, heads)
        atts = gather_ctx(after(att, cot))
        ids = jnp.stack([z, f]).astype(jnp.int32)
        hidden, n2_all, att_all = out_norm(ids, atts, wos, xs, gain2[None, :], nz, n_fsdp)
        quarter = rows_all // TILE // 4
        *held, far1, near1 = ffn(f_id, n2_all, cot, w_gu, wd, n_fsdp, quarter, ())
        act, gg, ug, far0, near0 = ffn(f_id, n2_all, cot, w_gu, wd, n_fsdp, 0, tuple(held))
        n2_grad = reduce_ctx((far0, far1), (near0, near1))

        fourth = rows_all // 4

        def four(left, right):
            cut = [left[j * fourth : (j + 1) * fourth] for j in range(4)]
            low = [right(v).astype(BF) for v in cut]
            return (low[2], low[3]), (low[0], low[1])

        gg = after(gg, far0, near0)
        e_gu = terms(n2_all, [gg, ug], n_ctx, n_fsdp)
        act_late = after(act, e_gu)
        e_down = mm_tn(act_late, cot, BF)
        out_far, out_near = four(after(act, e_down), lambda v: mm(v, wd))
        e_gu = reduce_square(e_gu, f, None)
        down_slot = (z ^ f ^ (p * (n_fsdp // 2))) % n_fsdp
        e_down = reduce_square(e_down.reshape(n_fsdp, ff_bp, width), down_slot, n2_grad)
        e_down = e_down.astype(BF)

        r2 = lax.rsqrt(jnp.mean(hidden * hidden, axis=-1, keepdims=True) + EPS)
        weighted = n2_grad * gain2[None, :]
        hidden_grad = (
            cotangent[0].astype(F32)
            + r2 * weighted
            - hidden * (r2 * r2 * r2 * jnp.mean(weighted * hidden, axis=-1, keepdims=True))
        )
        branch = hidden_grad.astype(BF)
        pair_branch = jnp.concatenate([branch, swap(branch)], 0)
        wo_rel = jnp.concatenate(wo_mine, 0)
        agrads = mm_nt(pair_branch, wo_rel).astype(BF)

        def block_of(k):
            return cols(agrads, ((z ^ k) ^ f) * q_cols, q_cols)

        got = [block_of(0)] + [chip(block_of(k), k) for k in range(1, nz)]
        pair_late = after(pair_branch, *got)

        def columns_of(k):
            return cols(pair_late, ((z ^ k) * 2 + p) * q_cols, q_cols)

        sent = [columns_of(0)] + [chip(columns_of(k), k) for k in range(1, nz)]
        output = (hidden + reduce_ctx(out_far, out_near, got[1])).astype(BF)

        dqkv = attention_back(offs, ends, got, qm, kk, vv, lse, cos, sin, span, heads)
        n1_far, n1_near = four(dqkv, lambda v: mm_nt(v, wqkv))
        n1_grad = reduce_ctx(n1_far, n1_near)
        inputs = x_own.astype(F32)
        r1 = lax.rsqrt(jnp.mean(inputs * inputs, axis=-1, keepdims=True) + EPS)
        weighted = n1_grad * gain1[None, :]
        grad_in = (
            hidden_grad
            + r1 * weighted
            - inputs * (r1 * r1 * r1 * jnp.mean(weighted * inputs, axis=-1, keepdims=True))
        ).astype(BF)

        moves = []
        for ci in range(n_ctx):
            for fi in range(n_fsdp):
                held_by = ((ci // 2) ^ fi ^ ((ci % 2) * (n_fsdp // 2))) % n_fsdp
                moves.append((ci * n_fsdp + fi, held_by * n_ctx + ci))
        grad_down = lax.ppermute(e_down[:ff_b], both, moves)
        grad_down = after(grad_down, n1_grad).astype(F32)
        t_qkv = terms(n1_all, [after(dqkv, *n1_far, *n1_near)], n_ctx, n_fsdp)
        t_out = terms(att_all, sent, n_ctx, n_fsdp, joined=True)
        e_qkv = reduce_face(t_qkv, f)
        e_out = reduce_face(t_out, f)

        def split(v):
            high = lax.reduce_precision(v, 8, 7)
            return high.astype(BF), (v - high).astype(BF)

        def row_sums(e, w_rows):
            return split(
                jnp.sum(e.astype(F32) * w_rows.astype(F32), axis=-1, keepdims=True)
            )

        per = n_ctx // n_fsdp
        w_gu = [after(w, *n1_far, *n1_near) for w in w_gu]
        if len(w_gu) > n_fsdp:
            whole = w_gu[: n_fsdp - 1] + [jnp.concatenate(w_gu[n_fsdp - 1 :], 0)]
        else:
            whole = w_gu
        mine_gu = jnp.stack(
            [
                lax.dynamic_index_in_dim(
                    w.reshape(2, per, n_fsdp, rows_b, ff_p), f, 2, keepdims=False
                )
                for w in whole
            ],
            0,
        )
        mine_gu = jnp.take(mine_gu, f ^ jnp.arange(n_fsdp, dtype=jnp.int32), axis=0)
        mine_gu = mine_gu.transpose(0, 2, 1, 3, 4).reshape(n_ctx, 2 * rows_b, ff_p)
        high, low = row_sums(e_gu, mine_gu)
        spot = jnp.arange(ff_p, dtype=jnp.int32)[None, None, :]
        ship = jnp.where(spot == ff_b, high, jnp.where(spot == ff_b + 1, low, e_gu.astype(BF)))
        recv_gu = lax.all_to_all(ship, "ctx", 0, 0, tiled=True)

        mine_qkv = wqkv.reshape(n_ctx, n_fsdp, rows_b, q_cols + 128)
        mine_qkv = lax.dynamic_index_in_dim(mine_qkv, f, 1, keepdims=False)
        high, low = row_sums(e_qkv, mine_qkv)
        gap = jnp.zeros((n_ctx, rows_b, 126), BF)
        order = jnp.arange(n_ctx, dtype=jnp.int32)
        e_out = jnp.take(e_out.astype(BF), ((order % 2) ^ p) * nz + order // 2, axis=0)
        ship = jnp.concatenate([e_qkv.astype(BF), high, low, gap, e_out], -1)
        recv_qkv = lax.all_to_all(after(ship, recv_gu), "ctx", 0, 0, tiled=True)
        recv_qkv = recv_qkv.astype(F32)
        my_row = (c * n_fsdp + f) * rows_b
        gain1_r = lax.dynamic_slice_in_dim(gain1, my_row, rows_b, 0)
        gain2_r = lax.dynamic_slice_in_dim(gain2, my_row, rows_b, 0)

        grad_gate, grad_up = assemble(recv_gu, n_fsdp, ff_b)
        sum_gu = jnp.sum(recv_gu[:, :, ff_b : ff_b + 2].astype(F32), (0, 2))
        grad_g2 = (sum_gu[:rows_b] + sum_gu[rows_b:]) / gain2_r
        grad_out = recv_qkv[:, :, q_cols + 256 :].transpose(1, 0, 2).reshape(rows_b, -1)
        grad_query = recv_qkv[:, :, :q_cols].transpose(1, 0, 2).reshape(rows_b, -1)
        share = n_ctx // KV_HEADS

        def lay_kv(start):
            part = recv_qkv[:, :, start : start + HEAD].reshape(KV_HEADS, share, rows_b, HEAD)
            return jnp.sum(part, 1).transpose(1, 0, 2).reshape(rows_b, -1)

        grad_key = lay_kv(q_cols)
        grad_value = lay_kv(q_cols + HEAD)
        grad_g1 = jnp.sum(recv_qkv[:, :, q_cols + 128 : q_cols + 130], (0, 2)) / gain1_r
        return (
            output[None],
            grad_in[None],
            grad_g1,
            grad_query,
            grad_key,
            grad_value,
            grad_out,
            grad_g2,
            grad_gate,
            grad_up,
            grad_down,
        )

    return body


def solution(mesh):
    body = make_body(mesh.shape["ctx"], mesh.shape["fsdp"])
    both = ("ctx", "fsdp")
    in_specs = (
        P("fsdp", "ctx", None),
        P("fsdp", "ctx", None),
        P("fsdp", None),
        P("fsdp", None),
        P("fsdp"),
        P("fsdp", None),
        P("fsdp", None),
        P("fsdp", None),
        P("fsdp", None),
        P("fsdp"),
        P("fsdp", None),
        P("fsdp", None),
        P("fsdp", None),
    )
    out_specs = (
        P("fsdp", "ctx", None),
        P("fsdp", "ctx", None),
        P(both),
        P(both, None),
        P(both, None),
        P(both, None),
        P(both, None),
        P(both),
        P(both, None),
        P(both, None),
        P(both, None),
    )
    return jax.shard_map(body, mesh=mesh, in_specs=in_specs, out_specs=out_specs, check_vma=False)
```

```python
import functools
import math

import jax
import jax.numpy as jnp
from jax import lax
from jax.experimental import pallas as pl
from jax.experimental.pallas import tpu as pltpu
from jax.sharding import PartitionSpec as P


HEADS = 32
KV_HEADS = 4
HEAD = 64
EPS = 1e-05
THETA = 10000.0
NEGATIVE = -1e30
BF = jnp.bfloat16
F32 = jnp.float32
TILE = 256
VMEM = pl.BlockSpec(memory_space=pltpu.VMEM)
SMEM = pl.BlockSpec(memory_space=pltpu.SMEM)
ANY = pl.BlockSpec(memory_space=pl.ANY)


def dot(left, right, dims, out=F32):
    return lax.dot_general(left, right, (dims, ((), ())), preferred_element_type=out)


def mm(left, right, out=F32):
    return dot(left, right, ((1,), (0,)), out)


def mm_nt(left, right, out=F32):
    return dot(left, right, ((1,), (1,)), out)


def mm_tn(left, right, out=F32):
    return dot(left, right, ((0,), (0,)), out)


def params(mb):
    return pltpu.CompilerParams(vmem_limit_bytes=mb << 20)


def cost(flops, moved, trans=0):
    return pl.CostEstimate(flops=int(flops), bytes_accessed=int(moved), transcendentals=int(trans))


def norm_qkv_body(n_x, n_f, shard, ids, *refs):
    xs = refs[:n_x]
    packs = refs[n_x : n_x + n_f]
    normed, qkv, w_all, gains, row, sems = refs[n_x + n_f :]
    me = ids[0]
    copies = []
    for k in range(n_f):
        at = me ^ k
        copies.append(
            pltpu.make_async_copy(
                packs[k].at[pl.ds(0, shard)],
                w_all.at[pl.ds(pl.multiple_of(at * shard, shard), shard)],
                sems.at[k],
            )
        )
        copies.append(
            pltpu.make_async_copy(packs[k].at[pl.ds(shard, 16)], gains.at[at], sems.at[n_f + k])
        )
    for copy in copies:
        copy.start()
    for copy in copies:
        copy.wait()
    for g in range(n_f):
        part = gains[g].astype(F32)
        for j in range(shard // 128):
            start = g * shard + j * 128
            row[0:1, start : start + 128] = part[j : j + 1, 0:128]
    tok = xs[0].shape[0]
    gain = row[...]
    for b in range(n_x):
        x = xs[b][...].astype(F32)
        r = lax.rsqrt(jnp.mean(x * x, axis=-1, keepdims=True) + EPS)
        normed[b * tok : (b + 1) * tok, :] = (x * r * gain).astype(BF)
    qkv[...] = mm(normed[...], w_all[...])


def norm_qkv(f_id, xs, packs, shard):
    n_x, n_f = len(xs), len(packs)
    tok, width = xs[0].shape
    cols = packs[0].shape[1]
    rows = n_x * tok
    return pl.pallas_call(
        functools.partial(norm_qkv_body, n_x, n_f, shard),
        in_specs=[SMEM] + [VMEM] * n_x + [ANY] * n_f,
        out_specs=[VMEM] * 4,
        out_shape=[
            jax.ShapeDtypeStruct((rows, width), BF),
            jax.ShapeDtypeStruct((rows, cols), F32),
            jax.ShapeDtypeStruct((width, cols), BF),
            jax.ShapeDtypeStruct((n_f, 16, cols), BF),
        ],
        scratch_shapes=[pltpu.VMEM((1, width), F32), pltpu.SemaphoreType.DMA((2 * n_f,))],
        compiler_params=params(40),
        cost_estimate=cost(2 * rows * width * cols, 4 * rows * width),
        name="norm_qkv",
    )(f_id, *xs, *packs)


def half_swap(x):
    lane = lax.broadcasted_iota(jnp.int32, x.shape, 1)
    return jnp.where(
        lane % HEAD < HEAD // 2, pltpu.roll(x, 128 - HEAD // 2, 1), pltpu.roll(x, HEAD // 2, 1)
    )


def bias_rows(ends, n_seq, i, keys):
    t = i * TILE + lax.broadcasted_iota(jnp.int32, (1, TILE), 1)
    first = jnp.zeros((1, TILE), jnp.int32)
    for s in range(n_seq):
        first = jnp.where(t >= ends[s], ends[s], first)
    u = lax.broadcasted_iota(jnp.int32, (keys, TILE), 0)
    return jnp.where((u <= t) & (u >= first), 0.0, NEGATIVE)


def attention_body(
    span, heads, n_seq, offs, ends, qkv, cos, sin, att, qm, kk, vv, lse, v_t, att_s, bias
):
    rows = qkv.shape[0]
    n_span = rows // span
    pairs = heads // 2
    q_cols = heads * HEAD

    def prepare(i, _):
        src = pl.ds(pl.multiple_of(offs[i], span), span)
        dst = pl.ds(pl.multiple_of(i * span, span), span)
        c, s = cos[src, :], sin[src, :]
        low = lax.broadcasted_iota(jnp.int32, (span, 128), 1) < HEAD
        for pr in range(pairs):
            x = qkv[src, pr * 128 : (pr + 1) * 128]
            q = (x * c + half_swap(x) * s).astype(BF).astype(F32) * (1.0 / math.sqrt(HEAD))
            qm[2 * pr, dst, :] = jnp.where(low, q, 0.0).astype(BF)
            qm[2 * pr + 1, dst, :] = jnp.where(low, 0.0, q).astype(BF)
        x = qkv[src, q_cols : q_cols + 128]
        kv = x * jnp.where(low, c, 1.0) + half_swap(x) * jnp.where(low, s, 0.0)
        other = pltpu.roll(kv, HEAD, 1)
        kk[dst, :] = jnp.where(low, kv, other).astype(BF)
        vv[dst, :] = jnp.where(low, other, kv).astype(BF)
        return 0

    lax.fori_loop(0, n_span, prepare, 0)
    v_t[...] = jnp.transpose(vv[...].astype(F32))[0:HEAD, :].astype(BF)
    for i in range(rows // TILE):
        keys = (i + 1) * TILE
        bias[0:keys, :] = bias_rows(ends, n_seq, i, keys)

        def one(h):
            s = mm_nt(kk[0:keys, :], qm[h, i * TILE : (i + 1) * TILE, :]) + bias[0:keys, :]
            top = jnp.max(s, axis=0, keepdims=True)
            e = jnp.exp(s - top)
            total = jnp.sum(e, axis=0, keepdims=True)
            lse[h, 0:1, i * TILE : (i + 1) * TILE] = top + jnp.log(total)
            return mm(v_t[:, 0:keys], (e * (1.0 / total)).astype(BF))

        for pr in range(pairs):
            both = jnp.concatenate([one(2 * pr), one(2 * pr + 1)], axis=0)
            att_s[i * TILE : (i + 1) * TILE, pr * 128 : (pr + 1) * 128] = jnp.transpose(
                both
            ).astype(BF)

    def restore(i, _):
        src = pl.ds(pl.multiple_of(i * span, span), span)
        att[pl.ds(pl.multiple_of(offs[i], span), span), :] = att_s[src, :]
        return 0

    lax.fori_loop(0, n_span, restore, 0)


def attention(offs, ends, qkv, cos, sin, span, heads):
    rows = qkv.shape[0]
    return pl.pallas_call(
        functools.partial(attention_body, span, heads, ends.shape[0]),
        in_specs=[SMEM, SMEM, VMEM, VMEM, VMEM],
        out_specs=[VMEM] * 5,
        out_shape=[
            jax.ShapeDtypeStruct((rows, heads * HEAD), BF),
            jax.ShapeDtypeStruct((heads, rows, 128), BF),
            jax.ShapeDtypeStruct((rows, 128), BF),
            jax.ShapeDtypeStruct((rows, 128), BF),
            jax.ShapeDtypeStruct((heads, 1, rows), F32),
        ],
        scratch_shapes=[
            pltpu.VMEM((HEAD, rows), BF),
            pltpu.VMEM((rows, heads * HEAD), BF),
            pltpu.VMEM((rows, TILE), F32),
        ],
        compiler_params=params(40),
        cost_estimate=cost(3 * heads * rows * rows * 128, 8 << 20, heads * rows * rows),
        name="attention",
    )(offs, ends, qkv, cos, sin)


def attention_back_body(
    span, heads, n_seq, n_piece, offs, ends, *refs
):
    pieces = refs[:n_piece]
    qm, kk, vv, lse, cos, sin, out = refs[n_piece : n_piece + 7]
    sends = refs[n_piece + 7 : 2 * n_piece + 7]
    grad, agm, k_t, dq_s, dkk, dvv, bias = refs[2 * n_piece + 7 :]
    rows = grad.shape[0]
    tok = pieces[0].shape[0] // 2
    for q in range(2):
        for k in range(n_piece):
            at = (q * n_piece + k) * tok
            grad[at : at + tok, :] = pieces[k][q * tok : (q + 1) * tok, :]
    n_span = rows // span
    pairs = heads // 2
    q_cols = heads * HEAD

    def prepare(i, _):
        src = pl.ds(pl.multiple_of(offs[i], span), span)
        dst = pl.ds(pl.multiple_of(i * span, span), span)
        low = lax.broadcasted_iota(jnp.int32, (span, 128), 1) < HEAD
        for pr in range(pairs):
            x = grad[src, pr * 128 : (pr + 1) * 128].astype(F32)
            agm[2 * pr, dst, :] = jnp.where(low, x, 0.0).astype(BF)
            agm[2 * pr + 1, dst, :] = jnp.where(low, 0.0, x).astype(BF)
        return 0

    lax.fori_loop(0, n_span, prepare, 0)
    k_t[...] = jnp.transpose(kk[...].astype(F32))[0:HEAD, :].astype(BF)
    dkk[...] = jnp.zeros_like(dkk)
    dvv[...] = jnp.zeros_like(dvv)
    for i in range(rows // TILE):
        keys = (i + 1) * TILE
        here = slice(i * TILE, (i + 1) * TILE)
        bias[0:keys, :] = bias_rows(ends, n_seq, i, keys)

        def one(h):
            q = qm[h, here, :]
            a = agm[h, here, :]
            s = mm_nt(kk[0:keys, :], q) + bias[0:keys, :]
            prob = jnp.exp(s - lse[h, 0:1, here])
            pg = mm_nt(vv[0:keys, :], a)
            delta = jnp.sum(prob * pg, axis=0, keepdims=True)
            ds = (prob * (pg - delta)).astype(BF)
            dkk[0:keys, :] += mm(ds, q)
            dvv[0:keys, :] += mm(prob.astype(BF), a)
            return mm(k_t[:, 0:keys], ds)

        for pr in range(pairs):
            both = jnp.concatenate([one(2 * pr), one(2 * pr + 1)], axis=0)
            dq_s[here, pr * 128 : (pr + 1) * 128] = jnp.transpose(both) * (1.0 / math.sqrt(HEAD))

    def restore(i, _):
        src = pl.ds(pl.multiple_of(i * span, span), span)
        dst = pl.ds(pl.multiple_of(offs[i], span), span)
        c, s = cos[dst, :], sin[dst, :]
        low = lax.broadcasted_iota(jnp.int32, (span, 128), 1) < HEAD
        for pr in range(pairs):
            x = dq_s[src, pr * 128 : (pr + 1) * 128]
            out[dst, pr * 128 : (pr + 1) * 128] = (x * c - half_swap(x) * s).astype(BF)
        k = dkk[src, :]
        v = dvv[src, :]
        x = jnp.where(low, k + pltpu.roll(k, HEAD, 1), v + pltpu.roll(v, HEAD, 1))
        x = x * jnp.where(low, c, 1.0) - half_swap(x) * jnp.where(low, s, 0.0)
        out[dst, q_cols : q_cols + 128] = x.astype(BF)
        return 0

    lax.fori_loop(0, n_span, restore, 0)
    for q in range(2):
        for k in range(n_piece):
            at = (q * n_piece + k) * tok
            sends[k][q * tok : (q + 1) * tok, :] = out[at : at + tok, :]


def attention_back(offs, ends, pieces, qm, kk, vv, lse, cos, sin, span, heads):
    rows = kk.shape[0]
    return pl.pallas_call(
        functools.partial(attention_back_body, span, heads, ends.shape[0], len(pieces)),
        in_specs=[SMEM, SMEM] + [VMEM] * (6 + len(pieces)),
        out_specs=[VMEM] * (1 + len(pieces)),
        out_shape=[jax.ShapeDtypeStruct((rows, heads * HEAD + 128), BF)]
        + [jax.ShapeDtypeStruct((pieces[0].shape[0], heads * HEAD + 128), BF)] * len(pieces),
        scratch_shapes=[
            pltpu.VMEM((rows, heads * HEAD), BF),
            pltpu.VMEM((heads, rows, 128), BF),
            pltpu.VMEM((HEAD, rows), BF),
            pltpu.VMEM((rows, heads * HEAD), F32),
            pltpu.VMEM((rows, 128), F32),
            pltpu.VMEM((rows, 128), F32),
            pltpu.VMEM((rows, TILE), F32),
        ],
        compiler_params=params(48),
        cost_estimate=cost(8 * heads * rows * rows * 128, 8 << 20, heads * rows * rows),
        name="attention_back",
    )(offs, ends, *pieces, qm, kk, vv, lse, cos, sin)


def out_norm_body(nz, n_f, n_w, ids, *refs):
    atts = refs[: 2 * nz]
    ws = refs[2 * nz : 2 * nz + 2 * n_w]
    xs = refs[2 * nz + 2 * n_w : 4 * nz + 2 * n_w]
    gain, hidden, normed, left, w_mine, w_other, sems = refs[4 * nz + 2 * n_w :]
    w_all = (w_mine, w_other)
    z, f = ids[0], ids[1]
    cols = atts[0].shape[1]
    tok = xs[0].shape[0]
    copies = []
    for q in range(2):
        used = 0
        for k in range(n_f):
            done = 0
            while done < cols:
                piece = ws[q * n_w + used]
                deep = piece.shape[0]
                at = pl.multiple_of((f ^ k) * cols + done, 64)
                copies.append((piece, w_all[q].at[pl.ds(at, deep)]))
                done += deep
                used += 1
    for q in range(2):
        for k in range(nz):
            lanes = pl.ds(pl.multiple_of((z ^ k) * cols, 128), cols)
            for b in range(2 * nz):
                src = ((b // nz) ^ q) * nz + ((b % nz) ^ k)
                copies.append(
                    (
                        atts[q * nz + k].at[pl.ds(src * tok, tok)],
                        left.at[q, pl.ds(b * tok, tok), lanes],
                    )
                )
    copies = [
        pltpu.make_async_copy(src, dst, sems.at[i]) for i, (src, dst) in enumerate(copies)
    ]
    for copy in copies:
        copy.start()
    for copy in copies:
        copy.wait()
    per = TILE // tok
    g = gain[...]
    for b in range(2 * nz // per):
        at = slice(b * TILE, (b + 1) * TILE)
        acc = mm(left[0, at, :], w_mine[...]) + mm(left[1, at, :], w_other[...])
        for j in range(per):
            h = acc[j * tok : (j + 1) * tok, :] + xs[b * per + j][...].astype(F32)
            if b == 0 and j == 0:
                hidden[...] = h
            r = lax.rsqrt(jnp.mean(h * h, axis=-1, keepdims=True) + EPS)
            lo = b * TILE + j * tok
            normed[lo : lo + tok, :] = (h * r * g).astype(BF)


def out_norm(ids, atts, ws, xs, gain, nz, n_f):
    rows, cols = atts[0].shape
    tok, width = xs[0].shape
    return pl.pallas_call(
        functools.partial(out_norm_body, nz, n_f, len(ws) // 2),
        in_specs=[SMEM] + [ANY] * (2 * nz + len(ws)) + [VMEM] * (2 * nz + 1),
        out_specs=[VMEM] * 4,
        out_shape=[
            jax.ShapeDtypeStruct((tok, width), F32),
            jax.ShapeDtypeStruct((rows, width), BF),
            jax.ShapeDtypeStruct((2, rows, nz * cols), BF),
            jax.ShapeDtypeStruct((n_f * cols, width), BF),
        ],
        scratch_shapes=[
            pltpu.VMEM((n_f * cols, width), BF),
            pltpu.SemaphoreType.DMA((4 * nz * nz + len(ws),)),
        ],
        compiler_params=params(56),
        cost_estimate=cost(2 * rows * width * width, 20 << 20),
        name="out_norm",
    )(ids, *atts, *ws, *xs, gain)


def ffn_body(half, n_f, n_w, n_d, n_held, ids, normed, cot, *refs):
    ws = refs[:n_w]
    downs = refs[n_w : n_w + n_d]
    outs = refs[n_w + n_d + n_held :]
    act, gg, ug, far, near = outs[:5]
    if n_d > 1:
        wd, sems = outs[5:]

        @pl.when(pl.program_id(0) == 0)
        def _():
            step = wd.shape[0] // n_f
            copies, k, done = [], 0, 0
            for j in range(n_d):
                deep = downs[j].shape[0]
                at = pl.multiple_of((ids[0] ^ k) * step + done, 16)
                copies.append(pltpu.make_async_copy(downs[j], wd.at[pl.ds(at, deep)], sems.at[j]))
                done += deep
                if done == step:
                    k, done = k + 1, 0
            for copy in copies:
                copy.start()
            for copy in copies:
                copy.wait()
    else:
        wd = downs[0]
    f = ids[0]
    i = pl.program_id(0)
    gates = [w.at[0] for w in ws[:n_f]]
    ups = [w.at[1] for w in ws[: n_f - 1]]
    ups.append(ws[n_f - 1].at[1] if n_w == n_f else ws[n_f].at[0])
    depth = gates[0].shape[0]
    lanes = [pl.ds(pl.multiple_of((f ^ k) * depth, 128), depth) for k in range(n_f)]
    gate = mm(normed[:, lanes[0]], gates[0][...])
    up = mm(normed[:, lanes[0]], ups[0][...])
    for k in range(1, n_f):
        piece = normed[:, lanes[k]]
        gate = gate + mm(piece, gates[k][...])
        up = up + mm(piece, ups[k][...])
    grad = mm_nt(cot[...], wd[...])
    sig = 1.0 / (1.0 + jnp.exp(-gate))
    silu = gate * sig
    act[...] = (silu * up).astype(BF)
    g = (grad * up * sig * (1.0 + gate * (1.0 - sig))).astype(BF)
    u = (grad * silu).astype(BF)
    gg[...] = g
    ug[...] = u

    def emit(out):
        for k in range(n_f):
            out[:, lanes[k]] = (mm_nt(g, gates[k][...]) + mm_nt(u, ups[k][...])).astype(BF)

    @pl.when(i < half)
    def _():
        emit(far)

    @pl.when(i >= half)
    def _():
        emit(near)


def ffn(f_id, normed, cot, ws, downs, n_f, base, held):
    rows, width = normed.shape
    ff_p = sum(d.shape[0] for d in downs)
    count = rows // TILE // 2
    half = count // 2
    joins = len(downs) > 1

    def turn(i):
        other = jnp.where(i < half, count, 0)
        return (other + base + lax.rem(i, half), 0)

    tile_in = pl.BlockSpec((TILE, width), turn)
    tile_ff = pl.BlockSpec((TILE, ff_p), turn)
    first_held = 3 + len(ws) + len(downs)
    return pl.pallas_call(
        functools.partial(ffn_body, half, n_f, len(ws), len(downs), len(held)),
        grid=(count,),
        in_specs=[SMEM, tile_in, tile_in]
        + [VMEM] * len(ws)
        + [ANY if joins else VMEM] * len(downs)
        + [ANY] * len(held),
        out_specs=[tile_ff, tile_ff, tile_ff]
        + [
            pl.BlockSpec((TILE, width), lambda i: (jnp.minimum(i, half - 1), 0)),
            pl.BlockSpec((TILE, width), lambda i: (jnp.maximum(i - half, 0), 0)),
        ]
        + [VMEM] * joins,
        out_shape=[jax.ShapeDtypeStruct((rows, ff_p), BF)] * 3
        + [jax.ShapeDtypeStruct((rows // 4, width), BF)] * 2
        + [jax.ShapeDtypeStruct((ff_p, width), BF)] * joins,
        scratch_shapes=[pltpu.SemaphoreType.DMA((len(downs),))] * joins,
        input_output_aliases={first_held + j: j for j in range(len(held))},
        compiler_params=params(48),
        cost_estimate=cost(5 * rows * width * ff_p, 20 << 20),
        name="ffn",
    )(f_id, normed, cot, *ws, *downs, *held)


def norm_grad_body(n_piece, n_w, n_f, ids, *refs):
    pieces = refs[:n_piece]
    ws = refs[n_piece : n_piece + n_w]
    own, other, left = refs[n_piece + n_w :]
    f = ids[0]
    tok = own.shape[0]
    cols = pieces[0].shape[1]
    depth = own.shape[1] // n_f
    for k in range(n_piece):
        left[:, k * cols : (k + 1) * cols] = pieces[k][...]
    k, done = 0, 0
    for j in range(n_w):
        deep = ws[j].shape[0]
        lanes = pl.ds(pl.multiple_of((f ^ k) * depth + done, 128), deep)
        got = mm_nt(left[...], ws[j][...])
        own[:, lanes] = got[:tok]
        other[:, lanes] = got[tok:].astype(BF)
        done += deep
        if done == depth:
            k, done = k + 1, 0


def norm_grad(f_id, pieces, ws, n_f):
    rows, cols = pieces[0].shape
    width = sum(w.shape[0] for w in ws)
    return pl.pallas_call(
        functools.partial(norm_grad_body, len(pieces), len(ws), n_f),
        in_specs=[SMEM] + [VMEM] * (len(pieces) + len(ws)),
        out_specs=[VMEM] * 2,
        out_shape=[
            jax.ShapeDtypeStruct((rows // 2, width), F32),
            jax.ShapeDtypeStruct((rows // 2, width), BF),
        ],
        scratch_shapes=[pltpu.VMEM((rows, len(pieces) * cols), BF)],
        compiler_params=params(32),
        cost_estimate=cost(2 * rows * width * cols * len(pieces), 8 << 20),
        name="norm_grad",
    )(f_id, *pieces, *ws)


def terms_body(n_f, joined, left, *refs):
    if joined:
        pieces, out, whole = refs[:-2], refs[-2], refs[-1]
        n_piece, tok = len(pieces), pieces[0].shape[0] // 2

        @pl.when(pl.program_id(0) == 0)
        def _():
            for q in range(2):
                for k in range(n_piece):
                    at = (q * n_piece + k) * tok
                    whole[at : at + tok, :] = pieces[k][q * tok : (q + 1) * tok, :]

        rights = [whole]
    else:
        rights, out = refs[:-1], refs[-1]
    lt = left[...]
    rows_b = lt.shape[1] // n_f
    for j, right in enumerate(rights):
        total = mm_tn(lt, right[...]).astype(BF)
        for k in range(n_f):
            out[k, 0, j * rows_b : (j + 1) * rows_b, :] = total[k * rows_b : (k + 1) * rows_b, :]


def terms(left, rights, n_ctx, n_f, joined=False):
    stacked = left.ndim == 3
    rows = left.shape[-2]
    width = left.size // rows
    cols = rights[0].shape[1]
    lanes = width // n_ctx
    deep = (1 if joined else len(rights)) * lanes // n_f
    if stacked:
        per = n_ctx // 2
        spec = pl.BlockSpec((None, rows, lanes), lambda i: (i // per, 0, lax.rem(i, per)))
    else:
        spec = pl.BlockSpec((rows, lanes), lambda i: (0, i))
    return pl.pallas_call(
        functools.partial(terms_body, n_f, joined),
        grid=(n_ctx,),
        scratch_shapes=[pltpu.VMEM((rows, cols), BF)] if joined else [],
        in_specs=[spec] + [VMEM] * len(rights),
        out_specs=pl.BlockSpec((n_f, 1, deep, cols), lambda i: (0, i, 0, 0)),
        out_shape=jax.ShapeDtypeStruct((n_f, n_ctx, deep, cols), BF),
        compiler_params=params(40),
        cost_estimate=cost(2 * rows * width * cols * len(rights), 16 << 20),
        name="terms",
    )(left, *rights)


def assemble_body(n_f, ff_b, recv, gate, up):
    n_ctx, both_rows, ff_p = recv.shape
    rows = both_rows // 2
    step = ff_p // n_f
    for c in range(n_ctx):
        for k in range(n_f):
            at = (k * n_ctx + c) * ff_b
            gate[:, at : at + ff_b] = recv[c, 0:rows, k * step : k * step + ff_b].astype(F32)
            up[:, at : at + ff_b] = recv[c, rows:both_rows, k * step : k * step + ff_b].astype(F32)


def assemble(recv, n_f, ff_b):
    n_ctx, both_rows, _ = recv.shape
    return pl.pallas_call(
        functools.partial(assemble_body, n_f, ff_b),
        in_specs=[VMEM],
        out_specs=[VMEM] * 2,
        out_shape=[jax.ShapeDtypeStruct((both_rows // 2, n_ctx * n_f * ff_b), F32)] * 2,
        compiler_params=params(24),
        cost_estimate=cost(0, 6 << 20),
        name="assemble",
    )(recv)


def after(value, *others):
    return lax.optimization_barrier((value,) + others)[0]


def make_body(n_ctx, n_fsdp):
    nz = n_ctx // 2
    both = ("ctx", "fsdp")
    core_swap = [(i, i ^ 1) for i in range(n_ctx)]

    def swap(x):
        return lax.ppermute(x, "ctx", core_swap)

    def chip(x, k):
        return lax.ppermute(x, "ctx", [(i, i ^ (2 * k)) for i in range(n_ctx)])

    def face(x, k):
        return lax.ppermute(x, "fsdp", [(i, i ^ k) for i in range(n_fsdp)])

    def pairs(links):
        return [(2 * a + core, 2 * b + core) for a, b in links for core in (0, 1)]

    def gather_ctx(x):
        if nz == 4:
            two = chip(x, 2)
            near = lax.ppermute(x, "ctx", pairs([(1, 2), (2, 1)]))
            one = chip(x, 1)
            relay = lax.ppermute(two, "ctx", pairs([(2, 3), (1, 0)]))
            z = lax.axis_index("ctx") // 2
            three = jnp.where((z == 1) | (z == 2), near, relay)
            mine = [x, one, two, three]
        else:
            mine = [x] + [chip(x, k) for k in range(1, nz)]
        out = mine + [swap(m) for m in mine[:-1]]
        return out + [swap(mine[-1])]

    def reduce_ctx(far, near, wait=None):
        rows = 2 * near[0].shape[0] // nz
        sums = []
        for part in (1, 0):
            other = swap(far[part])
            sums += [
                near[part][k * rows : (k + 1) * rows].astype(F32)
                + other[k * rows : (k + 1) * rows].astype(F32)
                for k in range(nz // 2)
            ]
        sums = sums[nz // 2 :] + sums[: nz // 2]
        low = [v.astype(BF) for v in sums]
        if wait is not None:
            low = [after(v, wait) for v in low]
        if nz == 4:
            far_end = lax.ppermute(low[3], "ctx", pairs([(0, 1), (3, 2)]))
            middle = lax.ppermute(low[3], "ctx", pairs([(1, 2), (2, 1)]))
            one = chip(low[1], 1)
            two = chip((low[2].astype(F32) + far_end.astype(F32)).astype(BF), 2)
            parts = [one, middle, two]
        else:
            parts = [chip(low[k], k) for k in range(1, nz)]
        total = sums[0]
        for part in parts:
            total = total + part.astype(F32)
        return total

    def gather_face(x):
        if n_fsdp != 4:
            return [x] + [face(x, k) for k in range(1, n_fsdp)]
        one, two = face(x, 1), face(x, 2)
        half = x.shape[0] // 2
        return [x, one, two, face(two[:half], 1), face(one[half:], 2)]

    def slot_of(e, i):
        return lax.dynamic_index_in_dim(e, i, 0, keepdims=False)

    def reduce_face(e, slot):
        total = slot_of(e, slot).astype(F32)
        parts = [face(slot_of(e, slot ^ k), k) for k in range(1, n_fsdp)]
        for part in parts:
            total = total + part.astype(F32)
        return total

    def reduce_square(e, slot, wait):
        if n_fsdp != 4:
            return reduce_face(e, slot)
        half = e.shape[1] // 2
        corner = slot_of(e, slot ^ 3)
        low = face(corner[:half], 1)
        high = face(corner[half:], 2)
        if wait is not None:
            low, high = after(low, wait), after(high, wait)
        two = slot_of(e, slot ^ 2)
        one = slot_of(e, slot ^ 1)
        two = jnp.concatenate(
            [(two[:half].astype(F32) + low.astype(F32)).astype(BF), two[half:]], 0
        )
        one = jnp.concatenate(
            [one[:half], (one[half:].astype(F32) + high.astype(F32)).astype(BF)], 0
        )
        parts = [face(one, 1), face(two, 2)]
        total = slot_of(e, slot).astype(F32)
        for part in parts:
            total = total + part.astype(F32)
        return total

    def body(
        tokens,
        cotangent,
        lengths,
        span_order,
        gain_attn,
        w_query,
        w_key,
        w_value,
        w_out,
        gain_ffn,
        w_gate,
        w_up,
        w_down,
    ):
        c = lax.axis_index("ctx")
        f = lax.axis_index("fsdp")
        z = c // 2
        p = c % 2
        tok = tokens.shape[1]
        span = tok // 2
        width = tokens.shape[2]
        rows_all = n_ctx * tok
        q_cols = HEADS * HEAD // n_ctx
        heads = HEADS // n_ctx
        kv = c * KV_HEADS // n_ctx
        ff = w_gate.shape[1]
        ff_c = ff // n_ctx
        ff_b = ff_c // n_fsdp
        ff_p = -(-ff_c // 128) * 128
        ff_bp = ff_p // n_fsdp
        shard = w_query.shape[0]
        rows_b = width // (n_ctx * n_fsdp)

        spans = jnp.arange(span_order.shape[1], dtype=jnp.int32)
        dealt = jnp.sum(
            jnp.where(span_order[0][None, :] == spans[:, None], spans[None, :], 0), axis=1
        )
        dev = dealt // 2
        offs = ((((dev % 2) ^ p) * nz + ((dev // 2) ^ z)) * 2 + dealt % 2) * span
        offs = offs.astype(jnp.int32)
        ends = jnp.cumsum(lengths[0]).astype(jnp.int32)
        starts = ends - lengths[0]
        row = jnp.arange(rows_all, dtype=jnp.int32)
        block = row // tok
        slot = (((block % nz) ^ z) * 2 + (p ^ (block // nz))) * 2 + (row % tok) // span
        chosen = jnp.sum(
            jnp.where(slot[:, None] == spans[None, :], span_order[0][None, :], 0), axis=1
        )
        anchor = chosen * span + row % span
        segment = jnp.sum((anchor[:, None] >= ends[None, :]).astype(jnp.int32), axis=1)
        first = jnp.sum(
            jnp.where(
                segment[:, None] == jnp.arange(ends.shape[0], dtype=jnp.int32)[None, :],
                starts[None, :],
                0,
            ),
            axis=1,
        )
        pos = (anchor - first).astype(F32)
        lane = jnp.arange(128, dtype=jnp.int32)
        inverse = THETA ** (-((lane % (HEAD // 2)).astype(F32) * 2.0 / HEAD))
        angles = pos[:, None] * inverse[None, :]
        sign = jnp.where(lane % HEAD < HEAD // 2, -1.0, 1.0).astype(F32)
        cos = jnp.cos(angles)
        sin = jnp.sin(angles) * sign[None, :]

        x_own = tokens[0]
        xs = gather_ctx(x_own)

        def cols(w, start, size):
            return lax.dynamic_slice_in_dim(w, start, size, 1)

        chunks = shard // 128
        gains = jnp.concatenate(
            [gain_attn.reshape(chunks, 128), gain_ffn.reshape(chunks, 128)], axis=1
        )
        gains = jnp.pad(gains, ((0, 16 - chunks), (0, q_cols + 128 - 256)))
        pack = jnp.concatenate(
            [
                jnp.concatenate(
                    [
                        cols(w_query, c * q_cols, q_cols),
                        cols(w_key, kv * HEAD, HEAD),
                        cols(w_value, kv * HEAD, HEAD),
                    ],
                    1,
                ),
                gains,
            ],
            0,
        )
        packs = [pack] + [face(pack, k) for k in range(1, n_fsdp)]
        wo_own = lax.dynamic_slice_in_dim(w_out, p * q_cols, q_cols, 0)
        wo_mine = gather_face(wo_own)

        def slices(w):
            gap = jnp.zeros((shard, ff_bp - ff_b), BF)
            out = []
            for k in range(n_fsdp):
                out += [cols(w, k * (ff // n_fsdp) + c * ff_b, ff_b), gap]
            return jnp.concatenate(out, 1)

        gu_own = jnp.stack([slices(w_gate), slices(w_up)], 0)
        w_gu = gather_face(gu_own)
        wd_own = jnp.pad(
            lax.dynamic_slice_in_dim(w_down, c * ff_b, ff_b, 0), ((0, ff_bp - ff_b), (0, 0))
        )
        wd_parts = gather_face(wd_own)
        wos = wo_mine + [swap(w) for w in wo_mine]

        back = []
        for k in range(nz):
            kv_k = (z ^ k) * KV_HEADS // nz
            back += [
                cols(w_query, ((z ^ k) * 2 + p) * q_cols, q_cols),
                cols(w_key, kv_k * HEAD, HEAD),
                cols(w_value, kv_k * HEAD, HEAD),
            ]
        back = jnp.concatenate(back, 1)

        f_id = f.reshape(1).astype(jnp.int32)
        n1_all, qkv, wqkv, gains_all = norm_qkv(f_id, xs, packs, shard)
        gain1 = gains_all[:, :chunks, 0:128].reshape(width).astype(F32)
        gain2 = gains_all[:, :chunks, 128:256].reshape(width).astype(F32)

        cot_own = after(cotangent[0], *xs[:nz])
        cot = jnp.concatenate(gather_ctx(cot_own), 0)

        att, qm, kk, vv, lse = attention(offs, ends, qkv, cos, sin, span, heads)
        atts = gather_ctx(att)
        w_back = gather_face(after(back, *atts[:nz]))
        ids = jnp.stack([z, f]).astype(jnp.int32)
        hidden, n2_all, att_all, wo_mine_all = out_norm(
            ids, atts, wos, xs, gain2[None, :], nz, n_fsdp
        )
        quarter = rows_all // TILE // 4
        *held, far1, near1, wd = ffn(f_id, n2_all, cot, w_gu, wd_parts, n_fsdp, quarter, ())
        act, gg, ug, far0, near0 = ffn(f_id, n2_all, cot, w_gu, [wd], n_fsdp, 0, tuple(held))
        n2_grad = reduce_ctx((far0, far1), (near0, near1))

        fourth = rows_all // 4

        def four(left, right):
            cut = [left[j * fourth : (j + 1) * fourth] for j in range(4)]
            low = [right(v).astype(BF) for v in cut]
            return (low[2], low[3]), (low[0], low[1])

        gg = after(gg, far0, near0)
        e_gu = terms(n2_all, [gg, ug], n_ctx, n_fsdp)
        act_late = after(act, e_gu)
        e_down = mm_tn(act_late, cot, BF)
        out_far, out_near = four(after(act, e_down), lambda v: mm(v, wd))
        r2 = lax.rsqrt(jnp.mean(hidden * hidden, axis=-1, keepdims=True) + EPS)
        weighted = n2_grad * gain2[None, :]
        hidden_grad = (
            cotangent[0].astype(F32)
            + r2 * weighted
            - hidden * (r2 * r2 * r2 * jnp.mean(weighted * hidden, axis=-1, keepdims=True))
        )
        branch = hidden_grad.astype(BF)
        pair_branch = jnp.concatenate([branch, swap(branch)], 0)
        agrads = mm_nt(pair_branch, wo_mine_all).astype(BF)

        def block_of(k):
            return cols(agrads, (z ^ k) * q_cols, q_cols)

        got = [block_of(0)] + [chip(block_of(k), k) for k in range(1, nz)]
        e_gu = reduce_square(e_gu, f, agrads)
        down_slot = (z ^ f ^ (p * (n_fsdp // 2))) % n_fsdp
        e_down = reduce_square(e_down.reshape(n_fsdp, ff_bp, width), down_slot, got[1])
        e_down = e_down.astype(BF)

        pair_late = after(pair_branch, *got)

        def columns_of(k):
            return cols(pair_late, ((z ^ k) * 2 + p) * q_cols, q_cols)

        sent = [columns_of(0)] + [chip(columns_of(k), k) for k in range(1, nz)]
        output = (hidden + reduce_ctx(out_far, out_near, got[1])).astype(BF)

        dqkv, *sends = attention_back(offs, ends, got, qm, kk, vv, lse, cos, sin, span, heads)
        sends = [sends[0]] + [chip(sends[k], k) for k in range(1, nz)]
        n1_own, n1_other = norm_grad(f_id, sends, w_back, n_fsdp)
        n1_grad = n1_own + swap(n1_other).astype(F32)
        inputs = x_own.astype(F32)
        r1 = lax.rsqrt(jnp.mean(inputs * inputs, axis=-1, keepdims=True) + EPS)
        weighted = n1_grad * gain1[None, :]
        grad_in = (
            hidden_grad
            + r1 * weighted
            - inputs * (r1 * r1 * r1 * jnp.mean(weighted * inputs, axis=-1, keepdims=True))
        ).astype(BF)

        moves = []
        for ci in range(n_ctx):
            for fi in range(n_fsdp):
                held_by = ((ci // 2) ^ fi ^ ((ci % 2) * (n_fsdp // 2))) % n_fsdp
                moves.append((ci * n_fsdp + fi, held_by * n_ctx + ci))
        grad_down = lax.ppermute(e_down[:ff_b], both, moves)
        grad_down = after(grad_down, n1_grad).astype(F32)
        t_qkv = terms(n1_all, [dqkv], n_ctx, n_fsdp)
        t_out = terms(att_all, sent, n_ctx, n_fsdp, joined=True)
        e_qkv = reduce_face(t_qkv, f)
        e_out = reduce_face(t_out, f)

        def split(v):
            high = lax.reduce_precision(v, 8, 7)
            return high.astype(BF), (v - high).astype(BF)

        def row_sums(e, w_rows):
            return split(
                jnp.sum(e.astype(F32) * w_rows.astype(F32), axis=-1, keepdims=True)
            )

        per = n_ctx // n_fsdp
        w_gu = [after(w, dqkv) for w in w_gu]
        if len(w_gu) > n_fsdp:
            whole = w_gu[: n_fsdp - 1] + [jnp.concatenate(w_gu[n_fsdp - 1 :], 0)]
        else:
            whole = w_gu
        mine_gu = jnp.stack(
            [
                lax.dynamic_index_in_dim(
                    w.reshape(2, per, n_fsdp, rows_b, ff_p), f, 2, keepdims=False
                )
                for w in whole
            ],
            0,
        )
        mine_gu = jnp.take(mine_gu, f ^ jnp.arange(n_fsdp, dtype=jnp.int32), axis=0)
        mine_gu = mine_gu.transpose(0, 2, 1, 3, 4).reshape(n_ctx, 2 * rows_b, ff_p)
        high, low = row_sums(e_gu, mine_gu)
        spot = jnp.arange(ff_p, dtype=jnp.int32)[None, None, :]
        ship = jnp.where(spot == ff_b, high, jnp.where(spot == ff_b + 1, low, e_gu.astype(BF)))
        recv_gu = lax.all_to_all(ship, "ctx", 0, 0, tiled=True)

        mine_qkv = wqkv.reshape(n_ctx, n_fsdp, rows_b, q_cols + 128)
        mine_qkv = lax.dynamic_index_in_dim(mine_qkv, f, 1, keepdims=False)
        high, low = row_sums(e_qkv, mine_qkv)
        gap = jnp.zeros((n_ctx, rows_b, 126), BF)
        order = jnp.arange(n_ctx, dtype=jnp.int32)
        e_out = jnp.take(e_out.astype(BF), ((order % 2) ^ p) * nz + order // 2, axis=0)
        ship = jnp.concatenate([e_qkv.astype(BF), high, low, gap, e_out], -1)
        recv_qkv = lax.all_to_all(after(ship, recv_gu), "ctx", 0, 0, tiled=True)
        recv_qkv = recv_qkv.astype(F32)
        my_row = (c * n_fsdp + f) * rows_b
        gain1_r = lax.dynamic_slice_in_dim(gain1, my_row, rows_b, 0)
        gain2_r = lax.dynamic_slice_in_dim(gain2, my_row, rows_b, 0)

        grad_gate, grad_up = assemble(recv_gu, n_fsdp, ff_b)
        sum_gu = jnp.sum(recv_gu[:, :, ff_b : ff_b + 2].astype(F32), (0, 2))
        grad_g2 = (sum_gu[:rows_b] + sum_gu[rows_b:]) / gain2_r
        grad_out = recv_qkv[:, :, q_cols + 256 :].transpose(1, 0, 2).reshape(rows_b, -1)
        grad_query = recv_qkv[:, :, :q_cols].transpose(1, 0, 2).reshape(rows_b, -1)
        share = n_ctx // KV_HEADS

        def lay_kv(start):
            part = recv_qkv[:, :, start : start + HEAD].reshape(KV_HEADS, share, rows_b, HEAD)
            return jnp.sum(part, 1).transpose(1, 0, 2).reshape(rows_b, -1)

        grad_key = lay_kv(q_cols)
        grad_value = lay_kv(q_cols + HEAD)
        grad_g1 = jnp.sum(recv_qkv[:, :, q_cols + 128 : q_cols + 130], (0, 2)) / gain1_r
        return (
            output[None],
            grad_in[None],
            grad_g1,
            grad_query,
            grad_key,
            grad_value,
            grad_out,
            grad_g2,
            grad_gate,
            grad_up,
            grad_down,
        )

    return body


def solution(mesh):
    body = make_body(mesh.shape["ctx"], mesh.shape["fsdp"])
    both = ("ctx", "fsdp")
    in_specs = (
        P("fsdp", "ctx", None),
        P("fsdp", "ctx", None),
        P("fsdp", None),
        P("fsdp", None),
        P("fsdp"),
        P("fsdp", None),
        P("fsdp", None),
        P("fsdp", None),
        P("fsdp", None),
        P("fsdp"),
        P("fsdp", None),
        P("fsdp", None),
        P("fsdp", None),
    )
    out_specs = (
        P("fsdp", "ctx", None),
        P("fsdp", "ctx", None),
        P(both),
        P(both, None),
        P(both, None),
        P(both, None),
        P(both, None),
        P(both),
        P(both, None),
        P(both, None),
        P(both, None),
    )
    return jax.shard_map(body, mesh=mesh, in_specs=in_specs, out_specs=out_specs, check_vma=False)
```
